128 devices in a mesh: dp: 8 (over x, core), seq: 16 (over y, z).
Axes of the slice: x: 4, y: 4, z: 4, core: 2. Of those that a mesh axis runs over, the one named last changes fastest.
Arguments:
- q_raw: bfloat16 [8, 2048, 4096], P('dp', 'seq'), may hold values from -64 to 64
- k_raw: bfloat16 [8, 2048, 4096], P('dp', 'seq'), may hold values from -64 to 64
- values: bfloat16 [8, 2048, 4096], P('dp', 'seq'), may hold values from -6 to 6
- grad_out: bfloat16 [8, 2048, 4096], P('dp', 'seq'), may hold values from -6 to 6
- q_gain: float32 [4096], replicated, may hold values from 0.1 to 1.9
- k_gain: float32 [4096], replicated, may hold values from 0.1 to 1.9
- lengths: int32 [8, 6], P('dp'), may hold values from 1 to 682, 2048 in all within a row
- positions: int32 [8, 3, 2048], P('dp', None, 'seq'), may hold values from 0 to 63
Outputs:
- attended: bfloat16 [8, 2048, 4096], P('dp', 'seq')
- grad_q: bfloat16 [8, 2048, 4096], P('dp', 'seq')
- grad_k: bfloat16 [8, 2048, 4096], P('dp', 'seq')
- grad_v: bfloat16 [8, 2048, 4096], P('dp', 'seq')
- grad_q_gain: float32 [4096], replicated
- grad_k_gain: float32 [4096], replicated
The draws below stay inside these ranges and needn't reach their ends.
Inputs may be any that keep to these rules, and one draw needn't show every extreme that they name: `lengths`: the clips of a bucket lie end to end and fill its 2048 tokens.
All inputs are finite; a program needn't handle non-finite values.
Results may differ from the reference program's by a relative error of at most 0.012.
The reference program's roundings to bfloat16 on the way (of `weights`, `prob_half` and `dscore`) count: a program that leaves them out, or rounds other values in their place, can miss the bound.
Values may be sent and summed in bfloat16 or wider, within the bound.
No kernel may reach another device: no remote copies, remote signals or barrier semaphores. Data moves between devices by JAX's collectives and lax.ppermute only.
A program may use at most 128 MiB of HBM per device.

```python
import math
import jax
import jax.numpy as jnp
import numpy as np
from jax import lax

HEADS = 32
HEAD_DIM = 128
FEAT = 4096
TOKENS = 2048
CLIPS = 6
CLIP_MOST = 682
GRID = 64
N_DP = 8


def draw_pair(key):
    base = jax.random.fold_in(key, 11)
    shape = (N_DP, TOKENS, FEAT)
    query = jax.random.normal(jax.random.fold_in(base, 1), shape, jnp.float32)
    keys = jax.random.normal(jax.random.fold_in(base, 2), shape, jnp.float32)
    return (jnp.clip(query, -64.0, 64.0), jnp.clip(keys, -64.0, 64.0))


def draw_q_raw(key, part):
    return draw_pair(key)[0].astype(jnp.bfloat16)


def draw_k_raw(key, part):
    return draw_pair(key)[1].astype(jnp.bfloat16)


def plant(array, rng, least, top_value):
    place = [jax.random.randint(jax.random.fold_in(rng, axis), (), 0, length) for axis, length in enumerate(array.shape)]
    main_axis = array.shape.index(max(array.shape))
    beside = place[:main_axis] + [(place[main_axis] + 1) % array.shape[main_axis]] + place[main_axis + 1:]
    return array.at[tuple(place)].set(least).at[tuple(beside)].set(top_value)


def block_scale(rng, extent, pieces, least, top_value):
    factor_of, own = 1.0, jax.random.fold_in(rng, 6)
    for axis_at, parts in pieces:
        draws = jnp.exp(jax.random.uniform(jax.random.fold_in(own, axis_at), (parts,), jnp.float32, least / len(pieces), top_value / len(pieces)))
        factor_of = factor_of * jnp.repeat(draws, extent[axis_at] // parts).reshape([-1 if axis == axis_at else 1 for axis in range(len(extent))])
    return factor_of


def length_profile(amount, total, most, skew):
    weights = [(1 << 20) // math.isqrt(standing ** skew) + 1 for standing in range(2, amount + 1)]
    surplus, counts = total - most - (amount - 1), [1] * (amount - 1)
    while surplus > 0:
        free = [i for i in range(amount - 1) if counts[i] < most]
        pool, budget = sum([weights[i] for i in free]), surplus
        for i in free:
            extra = min(most - counts[i], max(1, budget * weights[i] // pool), surplus)
            counts[i] = counts[i] + extra
            surplus = surplus - extra
    return np.array([most] + counts)


def ragged(rng, number_of, total, most, skew):
    if number_of == 2:
        one = jax.random.randint(rng, (), max(1, total - most), min(most, total - 1) + 1)
        return jnp.stack([one, total - one])
    sizes = jnp.asarray(length_profile(number_of, total, most, skew), jnp.int32)
    pairs = (number_of - 1) // 2
    source_of, sink = sizes[1:1 + 2 * pairs:2], sizes[2:2 + 2 * pairs:2]
    slack = jnp.minimum(source_of - 1, most - sink)
    moved = jax.random.randint(jax.random.fold_in(rng, 1), (pairs,), 0, 1 << 20) % (slack + 1)
    sizes = sizes.at[1:1 + 2 * pairs:2].set(source_of - moved).at[2:2 + 2 * pairs:2].set(sink + moved)
    return sizes[jax.random.permutation(jax.random.fold_in(rng, 2), number_of)]


def noise(own_key, shape, scale, limit, shards=(), held_as=jnp.bfloat16):
    factor_of = block_scale(own_key, shape, shards, -0.22, 0.18) if shards else 1.0
    entries = jax.random.normal(own_key, shape, jnp.float32) * scale * factor_of
    return jnp.minimum(jnp.maximum(entries, -limit), limit).astype(held_as)


def setup_inputs(seed: int = 0) -> dict:
    arg_keys = jax.random.split(jax.random.key(seed), 9)
    q_raw = draw_q_raw(jax.random.fold_in(arg_keys[8], 71), 0)
    k_raw = draw_k_raw(jax.random.fold_in(arg_keys[8], 71), 0)
    values = noise(arg_keys[2], (N_DP, TOKENS, FEAT), 1.0, 6.0, ((0, 8), (1, 16)))
    grad_out = noise(arg_keys[3], (N_DP, TOKENS, FEAT), 1.0, 6.0, ((0, 8), (1, 16)))
    q_gain = jnp.clip(1.0 + 0.18 * jax.random.normal(arg_keys[4], (FEAT,), jnp.float32), 0.1, 1.9)
    k_gain = jnp.clip(1.0 + 0.18 * jax.random.normal(arg_keys[5], (FEAT,), jnp.float32), 0.1, 1.9)
    lengths = jax.vmap(lambda own: ragged(own, CLIPS, TOKENS, CLIP_MOST, 2))(jax.random.split(arg_keys[6], N_DP)).reshape((N_DP, CLIPS)).astype(jnp.int32)
    positions = plant(jax.random.randint(arg_keys[7], (N_DP, 3, TOKENS), 0, GRID), jax.random.fold_in(arg_keys[7], 1), 0, GRID - 1).astype(jnp.int32)
    return {"q_raw": q_raw, "k_raw": k_raw, "values": values, "grad_out": grad_out, "q_gain": q_gain, "k_gain": k_gain, "lengths": lengths, "positions": positions}


epsilon = 1e-06

def product(form, left, right):
    return jnp.einsum(form, left.astype(jnp.float32), right.astype(jnp.float32))

def segment_ids(clip_lengths, tokens):
    boundary = jnp.cumsum(clip_lengths).astype(jnp.int32)
    places = jnp.arange(tokens, dtype=jnp.int32)
    return lax.optimization_barrier(jnp.sum((boundary[None, :] <= places[:, None]).astype(jnp.int32), axis=1)).astype(jnp.int32)

def rope_tables(position_rows, head_dim):
    half = head_dim // 2
    sixth = head_dim // 6
    first = half - 2 * sixth
    pairs = jnp.arange(half, dtype=jnp.int32)
    section = (pairs >= first).astype(jnp.int32) + (pairs >= first + sixth).astype(jnp.int32)
    begin = jnp.where(section == 0, 0, jnp.where(section == 1, first, first + sixth))
    number = jnp.where(section == 0, first, sixth)
    freqs = 10000.0 ** (-(pairs - begin).astype(jnp.float32) / number.astype(jnp.float32))
    picker = (section[None, :] == jnp.arange(3, dtype=jnp.int32)[:, None]).astype(jnp.float32) * freqs[None, :]
    angle = lax.dot_general(position_rows.astype(jnp.float32), picker, (((0,), (0,)), ((), ())), precision=lax.Precision.HIGHEST)
    cosine = jnp.cos(angle)
    sine = jnp.sin(angle)
    return (jnp.concatenate([cosine, cosine], axis=-1), jnp.concatenate([sine, sine], axis=-1))

def rotate_pairs(inputs, cosine, sine):
    half = inputs.shape[-1] // 2
    partner = jnp.concatenate([-inputs[..., half:], inputs[..., :half]], axis=-1)
    return inputs * cosine[:, None, :] + partner * sine[:, None, :]

def rotate_back(grads, cosine, sine):
    half = grads.shape[-1] // 2
    turned = grads * sine[:, None, :]
    return grads * cosine[:, None, :] + jnp.concatenate([turned[..., half:], -turned[..., :half]], axis=-1)

def attention_forward(query, keys, value_rows, segment, block, window, reach):
    count = query.shape[0]
    scale = query.shape[2] ** (-0.5)

    def one_block(index_block):
        start = (index_block * block).astype(jnp.int32)
        key_start = jnp.clip(start - reach, 0, count - window).astype(jnp.int32)
        query_block = lax.dynamic_slice_in_dim(query, start, block, 0)
        key_window = lax.dynamic_slice_in_dim(keys, key_start, window, 0)
        value_window = lax.dynamic_slice_in_dim(value_rows, key_start, window, 0)
        query_clip = lax.dynamic_slice_in_dim(segment, start, block, 0)
        key_clip = lax.dynamic_slice_in_dim(segment, key_start, window, 0)
        scores = product('qhd,khd->hqk', query_block, key_window) * scale
        live = (query_clip[:, None] == key_clip[None, :])[None]
        scores = jnp.where(live, scores, -1e+30)
        highest = lax.optimization_barrier(jnp.max(scores, axis=-1, keepdims=True))
        expon = jnp.exp(scores - highest)
        totals = lax.optimization_barrier(jnp.sum(expon, axis=-1, keepdims=True))
        weights = (expon / totals).astype(jnp.bfloat16)
        output = product('hqk,khd->qhd', weights, value_window)
        return (output, (highest + jnp.log(totals))[..., 0])
    outputs, logsum = lax.map(one_block, jnp.arange(count // block, dtype=jnp.int32))
    return (outputs.reshape(query.shape), logsum)

def attention_backward(query, keys, value_rows, context, cotangent, logsum, segment, block, window, reach):
    count = query.shape[0]
    scale = query.shape[2] ** (-0.5)
    delta = lax.optimization_barrier(jnp.sum(cotangent.astype(jnp.float32) * context.astype(jnp.float32), axis=-1))

    def one_block(carry, inputs):
        key_acc, value_acc = carry
        index_block, block_logsum = inputs
        start = (index_block * block).astype(jnp.int32)
        key_start = jnp.clip(start - reach, 0, count - window).astype(jnp.int32)
        query_block = lax.dynamic_slice_in_dim(query, start, block, 0)
        cot_block = lax.dynamic_slice_in_dim(cotangent, start, block, 0)
        delta_block = lax.dynamic_slice_in_dim(delta, start, block, 0)
        key_window = lax.dynamic_slice_in_dim(keys, key_start, window, 0)
        value_window = lax.dynamic_slice_in_dim(value_rows, key_start, window, 0)
        query_clip = lax.dynamic_slice_in_dim(segment, start, block, 0)
        key_clip = lax.dynamic_slice_in_dim(segment, key_start, window, 0)
        scores = product('qhd,khd->hqk', query_block, key_window) * scale
        live = (query_clip[:, None] == key_clip[None, :])[None]
        probs = jnp.where(live, jnp.exp(scores - block_logsum[:, :, None]), 0.0)
        prob_half = probs.astype(jnp.bfloat16)
        value_grad = product('hqk,qhd->khd', prob_half, cot_block)
        dprob = product('qhd,khd->hqk', cot_block, value_window)
        dscore = (probs * (dprob - jnp.transpose(delta_block)[:, :, None]) * scale).astype(jnp.bfloat16)
        query_grad = product('hqk,khd->qhd', dscore, key_window)
        key_grad = product('hqk,qhd->khd', dscore, query_block)
        key_acc = lax.dynamic_update_slice_in_dim(key_acc, lax.dynamic_slice_in_dim(key_acc, key_start, window, 0) + key_grad, key_start, 0)
        value_acc = lax.dynamic_update_slice_in_dim(value_acc, lax.dynamic_slice_in_dim(value_acc, key_start, window, 0) + value_grad, key_start, 0)
        return ((key_acc, value_acc), query_grad)
    zeros = jnp.zeros(query.shape, jnp.float32)
    indices = jnp.arange(count // block, dtype=jnp.int32)
    (key_acc, value_acc), query_grads = lax.scan(one_block, (zeros, zeros), (indices, logsum))
    return (query_grads.reshape(query.shape), key_acc, value_acc)

def norm_backward(grads_half, cosine, sine, scale_rows, hat_rows, gain_row):
    tokens = hat_rows.shape[0]
    grads = lax.optimization_barrier(grads_half).astype(jnp.float32)
    turned = rotate_back(grads, cosine, sine).reshape(tokens, -1)
    gain_part = lax.optimization_barrier(jnp.sum(turned * hat_rows, axis=0))
    lifted = turned * gain_row
    inner = lax.optimization_barrier(jnp.mean(lifted * hat_rows, axis=-1, keepdims=True))
    return ((scale_rows[:, None] * (lifted - hat_rows * inner)).astype(jnp.bfloat16), gain_part)

def reference(q_raw, k_raw, values, grad_out, q_gain, k_gain, lengths, positions):
    reach = CLIP_MOST
    block = min(512, TOKENS)
    window = min(TOKENS, block + 2 * reach)

    def replica(inputs):
        query_raw, key_raw, value_rows, cot_rows, clip_lengths, position_rows = inputs
        segment = segment_ids(clip_lengths, TOKENS)
        cosine, sine = rope_tables(position_rows, HEAD_DIM)
        query_float = query_raw.astype(jnp.float32)
        key_float = key_raw.astype(jnp.float32)
        query_scale = lax.rsqrt(lax.optimization_barrier(jnp.mean(query_float * query_float, axis=-1)) + epsilon)
        key_scale = lax.rsqrt(lax.optimization_barrier(jnp.mean(key_float * key_float, axis=-1)) + epsilon)
        query_hat = query_float * query_scale[:, None]
        key_hat = key_float * key_scale[:, None]
        query_rot = rotate_pairs((query_hat * q_gain).reshape(TOKENS, HEADS, HEAD_DIM), cosine, sine).astype(jnp.bfloat16)
        key_rot = rotate_pairs((key_hat * k_gain).reshape(TOKENS, HEADS, HEAD_DIM), cosine, sine).astype(jnp.bfloat16)
        value_heads = value_rows.reshape(TOKENS, HEADS, HEAD_DIM)
        context, logsum = attention_forward(query_rot, key_rot, value_heads, segment, block, window, reach)
        context_half = context.astype(jnp.bfloat16)
        cot_heads = cot_rows.reshape(TOKENS, HEADS, HEAD_DIM)
        query_grad, key_grad, value_grad = attention_backward(query_rot, key_rot, value_heads, context_half, cot_heads, logsum, segment, block, window, reach)
        query_input, query_part = norm_backward(query_grad.astype(jnp.bfloat16), cosine, sine, query_scale, query_hat, q_gain)
        key_input, key_part = norm_backward(key_grad.astype(jnp.bfloat16), cosine, sine, key_scale, key_hat, k_gain)
        return (context_half.reshape(TOKENS, FEAT), query_input, key_input, value_grad.astype(jnp.bfloat16).reshape(TOKENS, FEAT), query_part, key_part)
    attended, grad_q, grad_k, grad_v, query_parts, key_parts = lax.map(replica, (q_raw, k_raw, values, grad_out, lengths, positions))
    return (attended, grad_q, grad_k, grad_v, lax.optimization_barrier(jnp.sum(query_parts, axis=0)) / N_DP, lax.optimization_barrier(jnp.sum(key_parts, axis=0)) / N_DP)
```

```python
import functools
import math

import jax
import jax.numpy as jnp
import numpy as np
from jax import lax
from jax.experimental import pallas as pl
from jax.experimental.pallas import tpu as pltpu
from jax.sharding import PartitionSpec as P

HEAD_DIM = 128
HALF = HEAD_DIM // 2
EPSILON = 1e-06
APART = float(2**20)
QUERY_TILE = 256
KEY_STEP = 512
SLAB = 4 * HEAD_DIM
F32 = jnp.float32
BF16 = jnp.bfloat16


def frequency_row():
    sixth = HEAD_DIM // 6
    first = HALF - 2 * sixth
    pairs = np.arange(HALF)
    section = (pairs >= first).astype(int) + (pairs >= first + sixth).astype(int)
    begin = np.array([0, first, first + sixth])[section]
    count = np.array([first, sixth, sixth])[section]
    freqs = 10000.0 ** (-(pairs - begin) / count)
    return np.tile(freqs, 2)[None].astype(np.float32), (first, first + sixth)


def rotary_tables(rows, freqs):
    _, (second, third) = frequency_row()
    columns = rows.T
    tokens = columns.shape[0]
    lane = lax.broadcasted_iota(jnp.int32, (tokens, HEAD_DIM), 1)
    pair = lane & (HALF - 1)
    place = jnp.where(
        pair < second, columns[:, 0:1], jnp.where(pair < third, columns[:, 1:2], columns[:, 2:3])
    )
    angle = place * freqs
    return jnp.cos(angle), jnp.where(lane < HALF, -jnp.sin(angle), jnp.sin(angle))


def send_kernel(q_ref, k_ref, v_ref, g_ref, qg_ref, kg_ref, pos_ref, freq_ref, out_ref, cos_ref, sin_ref, qs_ref, ks_ref):
    tokens, feature = q_ref.shape
    rows = jnp.concatenate(
        [pos_ref[...].astype(F32), jnp.zeros((13, tokens), F32)], axis=0
    )
    cosine, sine = rotary_tables(rows, freq_ref[...])
    cos_ref[...] = cosine
    sin_ref[...] = sine
    members = out_ref.shape[0]
    local = feature // members // HEAD_DIM
    scales = []
    for ref, scale_ref in ((q_ref, qs_ref), (k_ref, ks_ref)):
        total = jnp.zeros((tokens, HEAD_DIM), F32)
        for h in range(feature // HEAD_DIM):
            part = ref[:, h * HEAD_DIM : (h + 1) * HEAD_DIM].astype(F32)
            total = total + part * part
        scale = lax.rsqrt(jnp.sum(total, axis=-1, keepdims=True) / feature + EPSILON)
        scale = jnp.broadcast_to(scale, (tokens, HEAD_DIM))
        scale_ref[...] = scale
        scales.append(scale)
    packed_rows = rows.astype(BF16)

    def one(j, carry):
        for h in range(local):
            at = pl.ds(pl.multiple_of((j * local + h) * HEAD_DIM, HEAD_DIM), HEAD_DIM)
            for a, (ref, gain_ref, scale_ref) in enumerate(((q_ref, qg_ref, qs_ref), (k_ref, kg_ref, ks_ref))):
                x = ref[:, at].astype(F32) * scale_ref[...] * gain_ref[:, at]
                turned = x * cos_ref[...] + pltpu.roll(x, HALF, 1) * sin_ref[...]
                out_ref[j, h * SLAB + a * tokens : h * SLAB + (a + 1) * tokens, :] = turned.astype(BF16)
            out_ref[j, h * SLAB + 2 * tokens : h * SLAB + 3 * tokens, :] = v_ref[:, at]
            out_ref[j, h * SLAB + 3 * tokens : h * SLAB + 4 * tokens, :] = g_ref[:, at]
        out_ref[j, local * SLAB : local * SLAB + 16, :] = packed_rows
        return carry

    lax.fori_loop(0, members, one, 0)


def dot(left, right, contract):
    return lax.dot_general(left, right, ((contract[0], contract[1]), ((), ())), preferred_element_type=F32)


def attention_kernel(len_ref, x_ref, freq_ref, out_ref, part_ref, kt, vt, keymask, querymask, s_ref, dk, dv):
    members = x_ref.shape[0]
    tok = HEAD_DIM
    tokens = members * tok
    local = (x_ref.shape[1] - 16) // SLAB
    clips = len_ref.shape[0]
    scale = HEAD_DIM ** (-0.5)
    factor = scale * math.log2(math.e)

    ends = []
    so_far = 0
    for c in range(clips):
        so_far = so_far + len_ref[c]
        ends.append(so_far)

    def masks(i, carry):
        token = lax.broadcasted_iota(jnp.int32, (tok, HEAD_DIM), 0) + i * tok
        lane = lax.broadcasted_iota(jnp.int32, (tok, HEAD_DIM), 1)
        clip = jnp.zeros((tok, HEAD_DIM), jnp.int32)
        for c in range(clips):
            clip = clip + (token >= ends[c]).astype(jnp.int32)
        own = clip == lane
        at = pl.ds(pl.multiple_of(i * tok, tok), tok)
        keymask[at, :] = jnp.where(own, -APART, 0.0).astype(BF16)
        querymask[at, :] = jnp.where(own, 0.0, 1.0).astype(BF16)
        for h in range(local):
            kt[h, :, at] = x_ref[i, h * SLAB + tok : h * SLAB + 2 * tok, :].T
            vt[h, :, at] = x_ref[i, h * SLAB + 2 * tok : h * SLAB + 3 * tok, :].T
            dk[h, at, :] = jnp.zeros((tok, HEAD_DIM), F32)
            dv[h, at, :] = jnp.zeros((tok, HEAD_DIM), F32)
        return carry

    lax.fori_loop(0, members, masks, 0)

    per = QUERY_TILE // tok
    step = KEY_STEP // tok

    def tile(i, carry):
        q0 = i * QUERY_TILE
        first, last = jnp.int32(0), jnp.int32(tokens)
        for c in range(clips):
            first = jnp.where(ends[c] <= q0, ends[c], first)
        for c in reversed(range(clips)):
            last = jnp.where(ends[c] >= q0 + QUERY_TILE, ends[c], last)
        low = first // tok
        count = (last - low * tok + KEY_STEP - 1) // KEY_STEP
        low = jnp.minimum(low, members - count * step)

        def block(h, a, start, number):
            return x_ref[pl.ds(start, number), h * SLAB + a * tok : h * SLAB + (a + 1) * tok, :].reshape(
                number * tok, HEAD_DIM
            )

        q_at = pl.ds(pl.multiple_of(q0, QUERY_TILE), QUERY_TILE)
        query_mask = querymask[q_at, :]
        queries = [block(h, 0, i * per, per) for h in range(local)]
        cots = [block(h, 3, i * per, per) for h in range(local)]
        wide = [jnp.concatenate([queries[h], query_mask], axis=1) for h in range(local)]

        def scores(j, highest):
            k0 = low + j * step
            k_at = pl.ds(pl.multiple_of(k0 * tok, tok), KEY_STEP)
            s_at = pl.ds(pl.multiple_of(j * KEY_STEP, KEY_STEP), KEY_STEP)
            key_mask = keymask[k_at, :]
            new = []
            for h in range(local):
                keys = jnp.concatenate([block(h, 1, k0, step), key_mask], axis=1)
                s = dot(keys, wide[h], ((1,), (1,)))
                s_ref[h, s_at, :] = s
                new.append(jnp.maximum(highest[h], jnp.max(s.reshape(KEY_STEP // 8, 8, QUERY_TILE), axis=0)))
            return tuple(new)

        lowest = jnp.full((8, QUERY_TILE), -4.0 * APART, F32)
        highest = lax.fori_loop(0, count, scores, (lowest,) * local)
        highest = [jnp.max(m, axis=0, keepdims=True) for m in highest]

        def forward(j, sums):
            k0 = low + j * step
            k_at = pl.ds(pl.multiple_of(k0 * tok, tok), KEY_STEP)
            s_at = pl.ds(pl.multiple_of(j * KEY_STEP, KEY_STEP), KEY_STEP)
            totals, outs = [], []
            for h in range(local):
                e = jnp.exp2((s_ref[h, s_at, :] - highest[h]) * factor)
                s_ref[h, s_at, :] = e
                totals.append(sums[0][h] + jnp.sum(e.reshape(KEY_STEP // 8, 8, QUERY_TILE), axis=0))
                outs.append(sums[1][h] + dot(vt[h, :, k_at], e.astype(BF16), ((1,), (0,))))
            return tuple(totals), tuple(outs)

        zero8 = jnp.zeros((8, QUERY_TILE), F32)
        zero_t = jnp.zeros((HEAD_DIM, QUERY_TILE), F32)
        totals, outs = lax.fori_loop(0, count, forward, ((zero8,) * local, (zero_t,) * local))
        inverse, deltas, cot_t = [], [], []
        for h in range(local):
            inv = 1.0 / jnp.sum(totals[h], axis=0, keepdims=True)
            attended = (outs[h] * inv).astype(BF16)
            turned = cots[h].T
            deltas.append(jnp.sum(attended.astype(F32) * turned.astype(F32), axis=0, keepdims=True))
            inverse.append(inv)
            cot_t.append(turned)
            out_ref[pl.ds(i * per, per), h * SLAB : h * SLAB + tok, :] = attended.T.reshape(per, tok, HEAD_DIM)

        def backward(j, sums):
            k0 = low + j * step
            k_at = pl.ds(pl.multiple_of(k0 * tok, tok), KEY_STEP)
            s_at = pl.ds(pl.multiple_of(j * KEY_STEP, KEY_STEP), KEY_STEP)
            new = []
            for h in range(local):
                prob = s_ref[h, s_at, :] * inverse[h]
                dprob = dot(block(h, 2, k0, step), cot_t[h], ((1,), (0,)))
                dscore = (prob * (dprob - deltas[h])).astype(BF16)
                dv[h, k_at, :] += dot(prob.astype(BF16), cots[h], ((1,), (0,)))
                dk[h, k_at, :] += dot(dscore, queries[h], ((1,), (0,)))
                new.append(sums[h] + dot(kt[h, :, k_at], dscore, ((1,), (0,))))
            return tuple(new)

        dq = lax.fori_loop(0, count, backward, (zero_t,) * local)
        for h in range(local):
            dq_tile = (dq[h] * scale).astype(BF16)
            out_ref[pl.ds(i * per, per), h * SLAB + tok : h * SLAB + 2 * tok, :] = dq_tile.T.reshape(
                per, tok, HEAD_DIM
            )
        return carry

    lax.fori_loop(0, tokens // QUERY_TILE, tile, 0)

    def finish(i, sums):
        at = pl.ds(pl.multiple_of(i * tok, tok), tok)
        cosine, sine = rotary_tables(x_ref[i, local * SLAB : local * SLAB + 16, :].astype(F32), freq_ref[...])
        new = []
        for h in range(local):
            dk_tile = (dk[h, at, :] * scale).astype(BF16)
            out_ref[i, h * SLAB + 2 * tok : h * SLAB + 3 * tok, :] = dk_tile
            out_ref[i, h * SLAB + 3 * tok : h * SLAB + 4 * tok, :] = dv[h, at, :].astype(BF16)
            dq_tile = out_ref[i, h * SLAB + tok : h * SLAB + 2 * tok, :]
            for a, grad in ((0, dq_tile), (1, dk_tile)):
                g = grad.astype(F32)
                p = x_ref[i, h * SLAB + a * tok : h * SLAB + (a + 1) * tok, :].astype(F32)
                g = g * cosine - pltpu.roll(g, HALF, 1) * sine
                p = p * cosine - pltpu.roll(p, HALF, 1) * sine
                new.append(sums[2 * h + a] + jnp.sum((g * p).reshape(tok // 8, 8, HEAD_DIM), axis=0))
        return tuple(new)

    sums = lax.fori_loop(0, members, finish, (jnp.zeros((8, HEAD_DIM), F32),) * (2 * local))
    part_ref[...] = jnp.concatenate(
        [jnp.sum(s, axis=0, keepdims=True) for s in sums] + [jnp.zeros((8 - 2 * local, HEAD_DIM), F32)], axis=0
    )


def receive_kernel(y_ref, q_ref, k_ref, qg_ref, kg_ref, cos_ref, sin_ref, qs_ref, ks_ref, att_ref, gq_ref, gk_ref, gv_ref, lift_q, lift_k):
    tokens, feature = q_ref.shape
    members = y_ref.shape[0]
    local = feature // members // HEAD_DIM
    groups = ((q_ref, qg_ref, qs_ref, gq_ref, lift_q), (k_ref, kg_ref, ks_ref, gk_ref, lift_k))

    def first(j, sums):
        sums = list(sums)
        for h in range(local):
            at = pl.ds(pl.multiple_of((j * local + h) * HEAD_DIM, HEAD_DIM), HEAD_DIM)
            att_ref[:, at] = y_ref[j, h * SLAB : h * SLAB + tokens, :]
            gv_ref[:, at] = y_ref[j, h * SLAB + 3 * tokens : h * SLAB + 4 * tokens, :]
            for a, (raw_ref, gain_ref, scale_ref, _, lift_ref) in enumerate(groups):
                g = y_ref[j, h * SLAB + (a + 1) * tokens : h * SLAB + (a + 2) * tokens, :].astype(F32)
                g = g * cos_ref[...] - pltpu.roll(g, HALF, 1) * sin_ref[...]
                lift = g * gain_ref[:, at]
                lift_ref[:, at] = lift
                sums[a] = sums[a] + lift * (raw_ref[:, at].astype(F32) * scale_ref[...])
        return tuple(sums)

    zero = jnp.zeros((tokens, HEAD_DIM), F32)
    sums = lax.fori_loop(0, members, first, (zero, zero))
    inner = [jnp.sum(s, axis=-1, keepdims=True) / feature for s in sums]

    def second(j, carry):
        for h in range(local):
            at = pl.ds(pl.multiple_of((j * local + h) * HEAD_DIM, HEAD_DIM), HEAD_DIM)
            for a, (raw_ref, _, scale_ref, grad_ref, lift_ref) in enumerate(groups):
                hat = raw_ref[:, at].astype(F32) * scale_ref[...]
                grad_ref[:, at] = (scale_ref[...] * (lift_ref[:, at] - hat * inner[a])).astype(BF16)
        return carry

    lax.fori_loop(0, members, second, 0)


def on_device(q_raw, k_raw, values, grad_out, q_gain, k_gain, lengths, positions):
    members = lax.axis_size("seq")
    replicas = lax.axis_size("dp")
    _, tok, feature = q_raw.shape
    local = feature // members // HEAD_DIM
    tokens = tok * members
    vmem = pl.BlockSpec(memory_space=pltpu.VMEM)
    smem = pl.BlockSpec(memory_space=pltpu.SMEM)
    freqs = jnp.asarray(frequency_row()[0])
    shape = jax.ShapeDtypeStruct
    wide = shape((tok, HEAD_DIM), F32)

    packet, cosine, sine, q_scale, k_scale = pl.pallas_call(
        send_kernel,
        out_shape=(shape((members, local * SLAB + 16, HEAD_DIM), BF16), wide, wide, wide, wide),
        in_specs=[vmem] * 8,
        out_specs=(vmem,) * 5,
        compiler_params=pltpu.CompilerParams(vmem_limit_bytes=48 << 20),
        cost_estimate=pl.CostEstimate(flops=40 << 20, bytes_accessed=9 << 20, transcendentals=0),
        name="send",
    )(q_raw[0], k_raw[0], values[0], grad_out[0], q_gain[None], k_gain[None], positions[0], freqs)

    got = lax.all_to_all(packet, "seq", 0, 0, tiled=True)

    back, part = pl.pallas_call(
        attention_kernel,
        out_shape=(shape((members, local * SLAB, HEAD_DIM), BF16), shape((8, HEAD_DIM), F32)),
        in_specs=[smem, vmem, vmem],
        out_specs=(vmem,) * 2,
        scratch_shapes=[
            pltpu.VMEM((local, HEAD_DIM, tokens), BF16),
            pltpu.VMEM((local, HEAD_DIM, tokens), BF16),
            pltpu.VMEM((tokens, HEAD_DIM), BF16),
            pltpu.VMEM((tokens, HEAD_DIM), BF16),
            pltpu.VMEM((local, tokens, QUERY_TILE), F32),
            pltpu.VMEM((local, tokens, HEAD_DIM), F32),
            pltpu.VMEM((local, tokens, HEAD_DIM), F32),
        ],
        compiler_params=pltpu.CompilerParams(vmem_limit_bytes=48 << 20),
        cost_estimate=pl.CostEstimate(flops=12 << 30, bytes_accessed=9 << 20, transcendentals=1 << 22),
        name="attention",
    )(lengths[0], got, freqs)

    returned = lax.all_to_all(back, "seq", 0, 0, tiled=True)

    for distance in (1, 2, 4):
        part = part + lax.ppermute(part, "dp", [(i, i ^ distance) for i in range(replicas)])
    mine = lax.broadcasted_iota(jnp.int32, (members, 1, 1), 0) == lax.axis_index("seq")
    every = jnp.where(mine, part[None], 0.0)
    for distance in (1, 2, 4, 8):
        every = every + lax.ppermute(every, "seq", [(i, i ^ distance) for i in range(members)])
    gains = every[:, : 2 * local].reshape(members, local, 2, HEAD_DIM)
    gain_out = [gains[:, :, a].reshape(feature) / (gain * replicas) for a, gain in enumerate((q_gain, k_gain))]

    outs = pl.pallas_call(
        receive_kernel,
        out_shape=(shape((tok, feature), BF16),) * 4,
        in_specs=[vmem] * 9,
        out_specs=(vmem,) * 4,
        scratch_shapes=[pltpu.VMEM((tok, feature), F32)] * 2,
        compiler_params=pltpu.CompilerParams(vmem_limit_bytes=48 << 20),
        cost_estimate=pl.CostEstimate(flops=40 << 20, bytes_accessed=10 << 20, transcendentals=0),
        name="receive",
    )(returned, q_raw[0], k_raw[0], q_gain[None], k_gain[None], cosine, sine, q_scale, k_scale)
    return tuple(o[None] for o in outs) + tuple(gain_out)


def solution(mesh):
    tokens_split = P("dp", "seq", None)
    return jax.shard_map(
        on_device,
        mesh=mesh,
        in_specs=(tokens_split,) * 4 + (P(), P(), P("dp", None), P("dp", None, "seq")),
        out_specs=(tokens_split,) * 4 + (P(), P()),
        check_vma=False,
    )
```

```python
import functools
import math

import jax
import jax.numpy as jnp
import numpy as np
from jax import lax
from jax.experimental import pallas as pl
from jax.experimental.pallas import tpu as pltpu
from jax.sharding import PartitionSpec as P

HEAD_DIM = 128
HALF = HEAD_DIM // 2
EPSILON = 1e-06
APART = float(2**20)
QUERY_TILE = 256
KEY_STEP = 512
SLAB = 4 * HEAD_DIM
F32 = jnp.float32
BF16 = jnp.bfloat16


GRID = 64


def rotary_table():
    sixth = HEAD_DIM // 6
    first = HALF - 2 * sixth
    table = np.zeros((3, GRID, HEAD_DIM))
    begin = 0
    for section, count in enumerate((first, sixth, sixth)):
        freqs = 10000.0 ** (-np.arange(count) / count)
        angle = np.arange(GRID)[:, None] * freqs[None]
        table[section, :, begin : begin + count] = np.cos(angle)
        table[section, :, HALF + begin : HALF + begin + count] = np.sin(angle)
        begin += count
    rest = table.reshape(3 * GRID, HEAD_DIM)
    terms = []
    for _ in range(3):
        terms.append(rest.astype(np.float32).astype(jnp.bfloat16))
        rest = rest - terms[-1].astype(np.float64)
    return np.concatenate(terms, axis=1)


def dot(left, right, contract):
    return lax.dot_general(left, right, ((contract[0], contract[1]), ((), ())), preferred_element_type=F32)


def rotary(rows, table):
    tokens = rows[0].shape[1]
    terms = dot(picks_of(rows), table, ((0,), (0,)))
    both = terms[:, :HEAD_DIM] + terms[:, HEAD_DIM : 2 * HEAD_DIM] + terms[:, 2 * HEAD_DIM :]
    other = pltpu.roll(both, HALF, 1)
    lower = lax.broadcasted_iota(jnp.int32, (tokens, HEAD_DIM), 1) < HALF
    return jnp.where(lower, both, other), jnp.where(lower, -other, both)


def double_table():
    sixth = HEAD_DIM // 6
    first = HALF - 2 * sixth
    table = np.zeros((3, GRID, 2, 2, HALF))
    begin = 0
    for section, count in enumerate((first, sixth, sixth)):
        angle = 2 * np.arange(GRID)[:, None] * 10000.0 ** (-np.arange(count) / count)[None]
        at = slice(begin, begin + count)
        table[section, :, 0, 0, at], table[section, :, 0, 1, at] = np.cos(angle), -np.cos(angle)
        table[section, :, 1, 0, at] = table[section, :, 1, 1, at] = np.sin(angle)
        begin += count
    table = table.reshape(3 * GRID, 2 * HEAD_DIM)
    high = table.astype(np.float32).astype(jnp.bfloat16)
    return np.concatenate([high, (table - high.astype(np.float64)).astype(np.float32).astype(jnp.bfloat16)], axis=1)


def picks_of(rows):
    number = lax.broadcasted_iota(jnp.int32, (GRID, rows[0].shape[1]), 0).astype(F32)
    return jnp.concatenate([jnp.where(number == row, 1.0, 0.0) for row in rows], axis=0).astype(BF16)


def columns(block):
    return pl.ds(pl.multiple_of(block * HEAD_DIM, HEAD_DIM), HEAD_DIM)


def send_kernel(q_hbm, k_hbm, v_hbm, g_hbm, qg_hbm, kg_hbm, pos_hbm, table_hbm, out_hbm, aside_ref, raw, gains, pos_ref, table_ref, stage, place, in_sem, small_sem, through_sem, out_sem, place_sem):
    tokens, feature = q_hbm.shape
    members = out_hbm.shape[0]
    local = feature // members // HEAD_DIM
    small = [
        pltpu.make_async_copy(source, target, small_sem.at[a])
        for a, (source, target) in enumerate(
            ((pos_hbm, pos_ref), (table_hbm, table_ref), (qg_hbm, gains.at[0]), (kg_hbm, gains.at[1]))
        )
    ]
    reads = [pltpu.make_async_copy(ref, raw.at[a], in_sem.at[a]) for a, ref in enumerate((q_hbm, k_hbm, v_hbm, g_hbm))]
    for copy in reads[:1] + small + reads[1:]:
        copy.start()
    small[0].wait()
    small[1].wait()
    rows = [pos_ref[a].astype(F32) for a in range(3)]
    aside_ref[0], aside_ref[1] = rotary(rows, table_ref[...])
    place[...] = jnp.concatenate(rows + [jnp.zeros((13, tokens), F32)], axis=0).astype(BF16)
    places = [
        pltpu.make_async_copy(place, out_hbm.at[j, local * SLAB : local * SLAB + 16, :], place_sem.at[j])
        for j in range(members)
    ]
    for copy in places:
        copy.start()
    for a in range(2):
        reads[a].wait()
        total = jnp.zeros((tokens, HEAD_DIM), F32)
        for h in range(feature // HEAD_DIM):
            part = raw[a, :, h * HEAD_DIM : (h + 1) * HEAD_DIM].astype(F32)
            total = total + part * part
        scale = lax.rsqrt(jnp.sum(total, axis=-1, keepdims=True) / feature + EPSILON)
        aside_ref[2 + a] = jnp.broadcast_to(scale, (tokens, HEAD_DIM))
    small[2].wait()
    small[3].wait()
    through = []
    for a in (2, 3):
        reads[a].wait()
        for j in range(members):
            for h in range(local):
                at = (j * local + h) * HEAD_DIM
                through.append(
                    pltpu.make_async_copy(
                        raw.at[a, :, at : at + HEAD_DIM],
                        out_hbm.at[j, h * SLAB + a * tokens : h * SLAB + (a + 1) * tokens, :],
                        through_sem.at[(j * local + h) * 2 + a - 2],
                    )
                )
                through[-1].start()

    def packet(j, h):
        return pltpu.make_async_copy(
            stage.at[j, h], out_hbm.at[j, h * SLAB : h * SLAB + 2 * tokens, :], out_sem.at[j, h]
        )

    def one(j, carry):
        for h in range(local):
            at = columns(j * local + h)
            for a in range(2):
                x = raw[a, :, at].astype(F32) * aside_ref[2 + a] * gains[a, :, at]
                turned = x * aside_ref[0] + pltpu.roll(x, HALF, 1) * aside_ref[1]
                stage[j, h, a * tokens : (a + 1) * tokens, :] = turned.astype(BF16)
            packet(j, h).start()
        return carry

    lax.fori_loop(0, members, one, 0, unroll=2)
    for copy in through + places:
        copy.wait()
    for j in range(members):
        for h in range(local):
            packet(j, h).wait()


def attention_kernel(len_ref, x_hbm, table_ref, out_hbm, x_ref, out_ref, qt, kt, vt, gt, keymask, s_ref, dk, dv, cos_ref, sin_ref, part_ref, in_sem, out_sem, part_sem):
    members = x_ref.shape[0]
    tok = HEAD_DIM
    tokens = members * tok
    local = (x_ref.shape[1] - 16) // SLAB
    clips = len_ref.shape[0]
    scale = HEAD_DIM ** (-0.5)
    factor = scale * math.log2(math.e)

    def read(i):
        return pltpu.make_async_copy(x_hbm.at[i], x_ref.at[i], in_sem.at[i])

    def start(i, carry):
        read(i).start()
        return carry

    lax.fori_loop(0, members, start, 0)
    ends = []
    so_far = 0
    for c in range(clips):
        so_far = so_far + len_ref[c]
        ends.append(so_far)

    def masks(i, carry):
        token = lax.broadcasted_iota(jnp.int32, (tok, HEAD_DIM), 0) + i * tok
        lane = lax.broadcasted_iota(jnp.int32, (tok, HEAD_DIM), 1)
        clip = jnp.zeros((tok, HEAD_DIM), jnp.int32)
        for c in range(clips):
            clip = clip + (token >= ends[c]).astype(jnp.int32)
        own = clip == lane
        at = pl.ds(pl.multiple_of(i * tok, tok), tok)
        keymask[at, :] = jnp.where(own, -APART, 0.0).astype(BF16)
        token = lax.broadcasted_iota(jnp.int32, (HEAD_DIM, tok), 1) + i * tok
        lane = lax.broadcasted_iota(jnp.int32, (HEAD_DIM, tok), 0)
        clip = jnp.zeros((HEAD_DIM, tok), jnp.int32)
        for c in range(clips):
            clip = clip + (token >= ends[c]).astype(jnp.int32)
        apart = jnp.where(clip == lane, 0.0, 1.0).astype(BF16)
        read(i).wait()
        rows = x_ref[i, local * SLAB : local * SLAB + 16, :].astype(F32)
        terms = dot(picks_of([rows[a : a + 1] for a in range(3)]), table_ref[...], ((0,), (0,)))
        both = terms[:, : 2 * HEAD_DIM] + terms[:, 2 * HEAD_DIM :]
        cos_ref[at, :], sin_ref[at, :] = both[:, :HEAD_DIM], both[:, HEAD_DIM:]
        for h in range(local):
            qt[h, :HEAD_DIM, at] = x_ref[i, h * SLAB : h * SLAB + tok, :].T
            qt[h, HEAD_DIM:, at] = apart
            gt[h, :, at] = x_ref[i, h * SLAB + 3 * tok : h * SLAB + 4 * tok, :].T
            kt[h, :, at] = x_ref[i, h * SLAB + tok : h * SLAB + 2 * tok, :].T
            vt[h, :, at] = x_ref[i, h * SLAB + 2 * tok : h * SLAB + 3 * tok, :].T
            dk[h, at, :] = jnp.zeros((tok, HEAD_DIM), F32)
            dv[h, at, :] = jnp.zeros((tok, HEAD_DIM), F32)
        return carry

    lax.fori_loop(0, members, masks, 0)

    per = QUERY_TILE // tok
    step = KEY_STEP // tok

    def tile(i, carry):
        q0 = i * QUERY_TILE
        first, last = jnp.int32(0), jnp.int32(tokens)
        for c in range(clips):
            first = jnp.where(ends[c] <= q0, ends[c], first)
        for c in reversed(range(clips)):
            last = jnp.where(ends[c] >= q0 + QUERY_TILE, ends[c], last)
        low = first // tok
        count = (last - low * tok + KEY_STEP - 1) // KEY_STEP
        low = jnp.minimum(low, members - count * step)

        def block(h, a, start, number):
            return x_ref[pl.ds(start, number), h * SLAB + a * tok : h * SLAB + (a + 1) * tok, :].reshape(
                number * tok, HEAD_DIM
            )

        q_at = pl.ds(pl.multiple_of(q0, QUERY_TILE), QUERY_TILE)
        queries = [block(h, 0, i * per, per) for h in range(local)]
        cots = [block(h, 3, i * per, per) for h in range(local)]


        def whole(number, heads):
            k0 = [low + j * step for j in range(number)]
            k_at = [pl.ds(pl.multiple_of(k * tok, tok), KEY_STEP) for k in k0]
            s, highest = {}, {}
            for h in heads:
                for j in range(number):
                    keys = jnp.concatenate([block(h, 1, k0[j], step), keymask[k_at[j], :]], axis=1)
                    s[h, j] = dot(keys, qt[h, :, q_at], ((1,), (0,)))
                    m = jnp.max(s[h, j].reshape(KEY_STEP // 8, 8, QUERY_TILE), axis=0)
                    highest[h] = m if j == 0 else jnp.maximum(highest[h], m)
            e, total, out = {}, {}, {}
            for h in heads:
                top = jnp.max(highest[h], axis=0, keepdims=True)
                for j in range(number):
                    e[h, j] = jnp.exp2((s[h, j] - top) * factor)
                    t = jnp.sum(e[h, j].reshape(KEY_STEP // 8, 8, QUERY_TILE), axis=0)
                    o = dot(vt[h, :, k_at[j]], e[h, j].astype(BF16), ((1,), (0,)))
                    total[h] = t if j == 0 else total[h] + t
                    out[h] = o if j == 0 else out[h] + o
            for h in heads:
                inv = 1.0 / jnp.sum(total[h], axis=0, keepdims=True)
                attended = (out[h] * inv).astype(BF16)
                delta = jnp.sum(attended.astype(F32) * gt[h, :, q_at].astype(F32), axis=0, keepdims=True)
                out_ref[pl.ds(i * per, per), h * SLAB : h * SLAB + tok, :] = attended.T.reshape(per, tok, HEAD_DIM)
                for j in range(number):
                    prob = e[h, j] * inv
                    dprob = dot(block(h, 2, k0[j], step), gt[h, :, q_at], ((1,), (0,)))
                    dscore = (prob * (dprob - delta)).astype(BF16)
                    dv[h, k_at[j], :] += dot(prob.astype(BF16), cots[h], ((1,), (0,)))
                    dk[h, k_at[j], :] += dot(dscore, queries[h], ((1,), (0,)))
                    d = dot(kt[h, :, k_at[j]], dscore, ((1,), (0,)))
                    dq = d if j == 0 else dq + d
                dq_tile = (dq * scale).astype(BF16)
                out_ref[pl.ds(i * per, per), h * SLAB + tok : h * SLAB + 2 * tok, :] = dq_tile.T.reshape(
                    per, tok, HEAD_DIM
                )

        for number in range(1, tokens // KEY_STEP + 1):

            @pl.when(count == number)
            def _():
                whole(number, range(local))

        return carry

    lax.fori_loop(0, tokens // QUERY_TILE, tile, 0)

    def write(i):
        return pltpu.make_async_copy(out_ref.at[i], out_hbm.at[i, : local * SLAB, :], out_sem.at[i])

    def finish(i, sums):
        at = pl.ds(pl.multiple_of(i * tok, tok), tok)
        cosine, sine = cos_ref[at, :], sin_ref[at, :]
        new = []
        for h in range(local):
            dk_tile = (dk[h, at, :] * scale).astype(BF16)
            out_ref[i, h * SLAB + 2 * tok : h * SLAB + 3 * tok, :] = dk_tile
            out_ref[i, h * SLAB + 3 * tok : h * SLAB + 4 * tok, :] = dv[h, at, :].astype(BF16)
        write(i).start()
        for h in range(local):
            for a, row in ((0, 1), (1, 2)):
                g = out_ref[i, h * SLAB + row * tok : h * SLAB + (row + 1) * tok, :].astype(F32)
                p = x_ref[i, h * SLAB + a * tok : h * SLAB + (a + 1) * tok, :].astype(F32)
                straight = g * p
                across = straight * cosine + g * pltpu.roll(p, HALF, 1) * sine
                plain, turned = sums[2 * h + a]
                new.append(
                    (
                        plain + jnp.sum(straight.reshape(tok // 8, 8, HEAD_DIM), axis=0),
                        turned + jnp.sum(across.reshape(tok // 8, 8, HEAD_DIM), axis=0),
                    )
                )
        return tuple(new)

    zero = jnp.zeros((8, HEAD_DIM), F32)
    sums = lax.fori_loop(0, members, finish, ((zero, zero),) * (2 * local))
    plain, turned = (jnp.concatenate([jnp.sum(s[n], axis=0, keepdims=True) for s in sums], axis=0) for n in range(2))
    plain = plain + pltpu.roll(plain, HALF, 1)
    turned = turned + pltpu.roll(turned, HALF, 1)
    lower = lax.broadcasted_iota(jnp.int32, plain.shape, 1) < HALF
    rest = 0.5 * (plain + jnp.where(lower, turned, -turned))
    terms = []
    for _ in range(3):
        terms.append(rest.astype(BF16).astype(F32))
        rest = rest - terms[-1]
    terms.append(jnp.zeros((16 - 6 * local, HEAD_DIM), F32))
    part_ref[...] = jnp.concatenate(terms, axis=0).astype(BF16)
    parts = [
        pltpu.make_async_copy(part_ref, out_hbm.at[i, local * SLAB : local * SLAB + 16, :], part_sem.at[i])
        for i in range(members)
    ]
    for copy in parts:
        copy.start()
    for i in range(members):
        write(i).wait()
        parts[i].wait()


def spread_kernel(y_hbm, att_hbm, gv_hbm, sem):
    tokens, feature = att_hbm.shape
    members = y_hbm.shape[0]
    local = feature // members // HEAD_DIM
    copies = []
    for j in range(members):
        for h in range(local):
            for a, (ref, row) in enumerate(((att_hbm, 0), (gv_hbm, 3))):
                at = (j * local + h) * HEAD_DIM
                copies.append(
                    pltpu.make_async_copy(
                        y_hbm.at[j, h * SLAB + row * tokens : h * SLAB + (row + 1) * tokens, :],
                        ref.at[:, at : at + HEAD_DIM],
                        sem.at[(j * local + h) * 2 + a],
                    )
                )
                copies[-1].start()
    for copy in copies:
        copy.wait()


def norm_kernel(which, y_ref, raw_ref, gain_ref, aside_ref, grad_hbm, lift_ref, stage, sem):
    tokens, feature = raw_ref.shape
    members = y_ref.shape[0]
    local = feature // members // HEAD_DIM
    parts = sem.shape[0]

    def first(j, total):
        for h in range(local):
            at = columns(j * local + h)
            g = y_ref[j, h * SLAB + (which + 1) * tokens : h * SLAB + (which + 2) * tokens, :].astype(F32)
            g = g * aside_ref[0] - pltpu.roll(g, HALF, 1) * aside_ref[1]
            lift = g * gain_ref[:, at]
            lift_ref[:, at] = lift
            total = total + lift * (raw_ref[:, at].astype(F32) * aside_ref[2 + which])
        return total

    total = lax.fori_loop(0, members, first, jnp.zeros((tokens, HEAD_DIM), F32), unroll=2)
    inner = jnp.sum(total, axis=-1, keepdims=True) / feature
    width = feature // parts
    copies = []
    for part in range(parts):
        for block in range(part * width // HEAD_DIM, (part + 1) * width // HEAD_DIM):
            at = slice(block * HEAD_DIM, (block + 1) * HEAD_DIM)
            hat = raw_ref[:, at].astype(F32) * aside_ref[2 + which]
            stage[:, at] = (aside_ref[2 + which] * (lift_ref[:, at] - hat * inner)).astype(BF16)
        at = slice(part * width, (part + 1) * width)
        copies.append(pltpu.make_async_copy(stage.at[:, at], grad_hbm.at[:, at], sem.at[part]))
        copies[-1].start()
    for copy in copies:
        copy.wait()


def on_device(q_raw, k_raw, values, grad_out, q_gain, k_gain, lengths, positions):
    members = lax.axis_size("seq")
    replicas = lax.axis_size("dp")
    _, tok, feature = q_raw.shape
    local = feature // members // HEAD_DIM
    tokens = tok * members
    vmem = pl.BlockSpec(memory_space=pltpu.VMEM)
    smem = pl.BlockSpec(memory_space=pltpu.SMEM)
    hbm = pl.BlockSpec(memory_space=pltpu.HBM)
    sems = pltpu.SemaphoreType.DMA
    table = jnp.asarray(rotary_table())
    shape = jax.ShapeDtypeStruct
    wide = shape((tok, HEAD_DIM), F32)
    whole = shape((members, local * SLAB + 16, HEAD_DIM), BF16)
    params = pltpu.CompilerParams(vmem_limit_bytes=48 << 20)

    packet, aside = pl.pallas_call(
        send_kernel,
        out_shape=(whole, shape((4, tok, HEAD_DIM), F32)),
        in_specs=[hbm] * 8,
        out_specs=(hbm, vmem),
        scratch_shapes=[
            pltpu.VMEM((4, tok, feature), BF16),
            pltpu.VMEM((2, 1, feature), F32),
            pltpu.VMEM((3, 1, tok), jnp.int32),
            pltpu.VMEM(table.shape, BF16),
            pltpu.VMEM((members, local, 2 * tok, HEAD_DIM), BF16),
            pltpu.VMEM((16, tok), BF16),
            sems((4,)),
            sems((4,)),
            sems((members * local * 2,)),
            sems((members, local)),
            sems((members,)),
        ],
        compiler_params=pltpu.CompilerParams(vmem_limit_bytes=60 << 20),
        cost_estimate=pl.CostEstimate(flops=40 << 20, bytes_accessed=9 << 20, transcendentals=0),
        name="send",
    )(q_raw[0], k_raw[0], values[0], grad_out[0], q_gain[None], k_gain[None], jnp.transpose(positions, (1, 0, 2)), table)

    got = lax.all_to_all(packet, "seq", 0, 0, tiled=True)

    back = pl.pallas_call(
        attention_kernel,
        out_shape=whole,
        in_specs=[smem, hbm, vmem],
        out_specs=hbm,
        scratch_shapes=[
            pltpu.VMEM((members, local * SLAB + 16, HEAD_DIM), BF16),
            pltpu.VMEM((members, local * SLAB, HEAD_DIM), BF16),
            pltpu.VMEM((local, 2 * HEAD_DIM, tokens), BF16),
            pltpu.VMEM((local, HEAD_DIM, tokens), BF16),
            pltpu.VMEM((local, HEAD_DIM, tokens), BF16),
            pltpu.VMEM((local, HEAD_DIM, tokens), BF16),
            pltpu.VMEM((tokens, HEAD_DIM), BF16),
            pltpu.VMEM((local, tokens, QUERY_TILE), F32),
            pltpu.VMEM((local, tokens, HEAD_DIM), F32),
            pltpu.VMEM((local, tokens, HEAD_DIM), F32),
            pltpu.VMEM((tokens, HEAD_DIM), F32),
            pltpu.VMEM((tokens, HEAD_DIM), F32),
            pltpu.VMEM((16, HEAD_DIM), BF16),
            sems((members,)),
            sems((members,)),
            sems((members,)),
        ],
        compiler_params=params,
        cost_estimate=pl.CostEstimate(flops=12 << 30, bytes_accessed=9 << 20, transcendentals=1 << 22),
        name="attention",
    )(lengths[0], got, jnp.asarray(double_table()))

    returned = lax.all_to_all(back, "seq", 0, 0, tiled=True)

    sums = sum(
        returned[:, local * SLAB + 2 * local * t : local * SLAB + 2 * local * (t + 1)].astype(F32) for t in range(3)
    )

    def add(value, distance):
        return value + lax.ppermute(value, "dp", [(i, i ^ distance) for i in range(replicas)])

    def norm(returned, which, raw, gain):
        return pl.pallas_call(
            functools.partial(norm_kernel, which),
            out_shape=shape((tok, feature), BF16),
            in_specs=[vmem] * 4,
            out_specs=hbm,
            scratch_shapes=[pltpu.VMEM((tok, feature), F32), pltpu.VMEM((tok, feature), BF16), sems((4,))],
            compiler_params=pltpu.CompilerParams(vmem_limit_bytes=24 << 20),
            cost_estimate=pl.CostEstimate(flops=20 << 20, bytes_accessed=4 << 20, transcendentals=0),
            name="receive",
        )(returned, raw[0], gain[None], aside)

    added = add(sums, 1)
    attended, grad_v = pl.pallas_call(
        spread_kernel,
        out_shape=(shape((tok, feature), BF16),) * 2,
        in_specs=[hbm],
        out_specs=(hbm, hbm),
        scratch_shapes=[sems((members * local * 2,))],
        compiler_params=params,
        cost_estimate=pl.CostEstimate(flops=0, bytes_accessed=8 << 20, transcendentals=0),
        name="receive_spread",
    )(returned)
    added, attended, grad_v, returned = lax.optimization_barrier((added, attended, grad_v, returned))
    sums = add(added, 2)
    grad_q = norm(returned, 0, q_raw, q_gain)
    sums, grad_q, returned = lax.optimization_barrier((sums, grad_q, returned))
    sums = add(sums, 4)
    grad_k = norm(returned, 1, k_raw, k_gain)
    gains = sums.reshape(members, local, 2, HEAD_DIM)
    gain_out = [gains[:, :, a].reshape(feature) / (gain * replicas) for a, gain in enumerate((q_gain, k_gain))]
    return tuple(o[None] for o in (attended, grad_q, grad_k, grad_v)) + tuple(gain_out)


def solution(mesh):
    tokens_split = P("dp", "seq", None)
    return jax.shard_map(
        on_device,
        mesh=mesh,
        in_specs=(tokens_split,) * 4 + (P(), P(), P("dp", None), P("dp", None, "seq")),
        out_specs=(tokens_split,) * 4 + (P(), P()),
        check_vma=False,
    )
```

```python
import functools
import math

import jax
import jax.numpy as jnp
import numpy as np
from jax import lax
from jax.experimental import pallas as pl
from jax.experimental.pallas import tpu as pltpu
from jax.sharding import PartitionSpec as P

HEAD_DIM = 128
HALF = HEAD_DIM // 2
EPSILON = 1e-06
APART = float(2**20)
QUERY_TILE = 256
KEY_STEP = 512
SLAB = 4 * HEAD_DIM
F32 = jnp.float32
BF16 = jnp.bfloat16


GRID = 64


def rotary_table():
    sixth = HEAD_DIM // 6
    first = HALF - 2 * sixth
    table = np.zeros((3, GRID, HEAD_DIM))
    begin = 0
    for section, count in enumerate((first, sixth, sixth)):
        freqs = 10000.0 ** (-np.arange(count) / count)
        angle = np.arange(GRID)[:, None] * freqs[None]
        table[section, :, begin : begin + count] = np.cos(angle)
        table[section, :, HALF + begin : HALF + begin + count] = np.sin(angle)
        begin += count
    rest = table.reshape(3 * GRID, HEAD_DIM)
    terms = []
    for _ in range(3):
        terms.append(rest.astype(np.float32).astype(jnp.bfloat16))
        rest = rest - terms[-1].astype(np.float64)
    return np.concatenate(terms, axis=1)


def dot(left, right, contract):
    return lax.dot_general(left, right, ((contract[0], contract[1]), ((), ())), preferred_element_type=F32)


def rotary(rows, table):
    tokens = rows[0].shape[1]
    terms = dot(picks_of(rows), table, ((0,), (0,)))
    both = terms[:, :HEAD_DIM] + terms[:, HEAD_DIM : 2 * HEAD_DIM] + terms[:, 2 * HEAD_DIM :]
    other = pltpu.roll(both, HALF, 1)
    lower = lax.broadcasted_iota(jnp.int32, (tokens, HEAD_DIM), 1) < HALF
    return jnp.where(lower, both, other), jnp.where(lower, -other, both)


def double_table():
    sixth = HEAD_DIM // 6
    first = HALF - 2 * sixth
    table = np.zeros((3, GRID, 2, 2, HALF))
    begin = 0
    for section, count in enumerate((first, sixth, sixth)):
        angle = 2 * np.arange(GRID)[:, None] * 10000.0 ** (-np.arange(count) / count)[None]
        at = slice(begin, begin + count)
        table[section, :, 0, 0, at], table[section, :, 0, 1, at] = np.cos(angle), -np.cos(angle)
        table[section, :, 1, 0, at] = table[section, :, 1, 1, at] = np.sin(angle)
        begin += count
    table = table.reshape(3 * GRID, 2 * HEAD_DIM)
    high = table.astype(np.float32).astype(jnp.bfloat16)
    return np.concatenate([high, (table - high.astype(np.float64)).astype(np.float32).astype(jnp.bfloat16)], axis=1)


def picks_of(rows):
    number = lax.broadcasted_iota(jnp.int32, (GRID, rows[0].shape[1]), 0).astype(F32)
    return jnp.concatenate([jnp.where(number == row, 1.0, 0.0) for row in rows], axis=0).astype(BF16)


def columns(block):
    return pl.ds(pl.multiple_of(block * HEAD_DIM, HEAD_DIM), HEAD_DIM)


def send_kernel(head, q_hbm, k_hbm, v_hbm, g_hbm, qg_hbm, kg_hbm, pos_hbm, table_hbm, *rest):
    if head == 0:
        out_hbm, aside_ref, raw, gains, pos_ref, table_ref, stage, in_sem, small_sem, out_sem = rest
    else:
        aside_ref, out_hbm, raw, gains, stage, in_sem, small_sem, out_sem = rest
    tokens, feature = q_hbm.shape
    members = out_hbm.shape[0]
    local = feature // members // HEAD_DIM
    sources = [(qg_hbm, gains.at[0]), (kg_hbm, gains.at[1])]
    if head == 0:
        sources += [(pos_hbm, pos_ref), (table_hbm, table_ref)]
    small = [pltpu.make_async_copy(source, target, small_sem.at[a]) for a, (source, target) in enumerate(sources)]
    reads = [pltpu.make_async_copy(ref, raw.at[a], in_sem.at[a]) for a, ref in enumerate((q_hbm, k_hbm, v_hbm, g_hbm))]
    for copy in small + reads:
        copy.start()
    for copy in small:
        copy.wait()
    if head == 0:
        rows = [pos_ref[a].astype(F32) for a in range(3)]
        aside_ref[0], aside_ref[1] = rotary(rows, table_ref[...])
        place = jnp.concatenate(rows + [jnp.zeros((13, tokens), F32)], axis=0).astype(BF16)
    for a in range(2):
        reads[a].wait()
        if head == 0:
            total = jnp.zeros((tokens, HEAD_DIM), F32)
            for h in range(feature // HEAD_DIM):
                part = raw[a, :, h * HEAD_DIM : (h + 1) * HEAD_DIM].astype(F32)
                total = total + part * part
            scale = lax.rsqrt(jnp.sum(total, axis=-1, keepdims=True) / feature + EPSILON)
            aside_ref[2 + a] = jnp.broadcast_to(scale, (tokens, HEAD_DIM))
    reads[2].wait()
    reads[3].wait()
    packets = []
    group = members // out_sem.shape[0]
    for j in range(members):
        at = slice((j * local + head) * HEAD_DIM, (j * local + head + 1) * HEAD_DIM)
        for a in range(2):
            x = raw[a, :, at].astype(F32) * aside_ref[2 + a] * gains[a, :, at]
            turned = x * aside_ref[0] + pltpu.roll(x, HALF, 1) * aside_ref[1]
            stage[j, a * tokens : (a + 1) * tokens, :] = turned.astype(BF16)
        for a in (2, 3):
            stage[j, a * tokens : (a + 1) * tokens, :] = raw[a, :, at]
        if head == 0:
            stage[j, SLAB:, :] = place
        if j % group == group - 1:
            some = slice(j + 1 - group, j + 1)
            packets.append(pltpu.make_async_copy(stage.at[some], out_hbm.at[some], out_sem.at[j // group]))
            packets[-1].start()
    for copy in packets:
        copy.wait()


def attention_kernel(head, len_ref, x_hbm, *rest):
    if head == 0:
        table_ref, out_hbm, sum_ref, angles_hbm, *rest = rest
    else:
        angles_hbm, before_ref, out_hbm, sum_ref, *rest = rest
    x_ref, out_ref, qt, kt, vt, gt, keymask, dk, dv, angles, in_sem, out_sem, angle_sem = rest
    members = x_ref.shape[0]
    tok = HEAD_DIM
    tokens = members * tok
    local = 1
    clips = len_ref.shape[0]
    scale = HEAD_DIM ** (-0.5)
    factor = scale * math.log2(math.e)

    group = members // in_sem.shape[0]

    def read(n):
        some = pl.ds(n * group, group)
        return pltpu.make_async_copy(x_hbm.at[some], x_ref.at[some], in_sem.at[n])

    for n in range(members // group):
        read(n).start()
    if head == 0:
        hand = pltpu.make_async_copy(angles, angles_hbm, angle_sem)
    else:
        hand = pltpu.make_async_copy(angles_hbm, angles, angle_sem)
        hand.start()
    ends = []
    so_far = 0
    for c in range(clips):
        so_far = so_far + len_ref[c]
        ends.append(so_far)

    def masks(i, carry):
        token = lax.broadcasted_iota(jnp.int32, (tok, HEAD_DIM), 0) + i * tok
        lane = lax.broadcasted_iota(jnp.int32, (tok, HEAD_DIM), 1)
        clip = jnp.zeros((tok, HEAD_DIM), jnp.int32)
        for c in range(clips):
            clip = clip + (token >= ends[c]).astype(jnp.int32)
        own = clip == lane
        at = pl.ds(pl.multiple_of(i * tok, tok), tok)
        keymask[at, :] = jnp.where(own, -APART, 0.0).astype(BF16)
        token = lax.broadcasted_iota(jnp.int32, (HEAD_DIM, tok), 1) + i * tok
        lane = lax.broadcasted_iota(jnp.int32, (HEAD_DIM, tok), 0)
        clip = jnp.zeros((HEAD_DIM, tok), jnp.int32)
        for c in range(clips):
            clip = clip + (token >= ends[c]).astype(jnp.int32)
        apart = jnp.where(clip == lane, 0.0, 1.0).astype(BF16)

        @pl.when(lax.rem(i, group) == 0)
        def _():
            read(i // group).wait()

        if head == 0:
            rows = x_ref[i, SLAB:, :].astype(F32)
            terms = dot(picks_of([rows[a : a + 1] for a in range(3)]), table_ref[...], ((0,), (0,)))
            angles[at, :] = terms[:, : 2 * HEAD_DIM] + terms[:, 2 * HEAD_DIM :]
        for h in range(local):
            qt[h, :HEAD_DIM, at] = x_ref[i, h * SLAB : h * SLAB + tok, :].T
            qt[h, HEAD_DIM:, at] = apart
            gt[h, :, at] = x_ref[i, h * SLAB + 3 * tok : h * SLAB + 4 * tok, :].T
            kt[h, :, at] = x_ref[i, h * SLAB + tok : h * SLAB + 2 * tok, :].T
            vt[h, :, at] = x_ref[i, h * SLAB + 2 * tok : h * SLAB + 3 * tok, :].T
            dk[h, at, :] = jnp.zeros((tok, HEAD_DIM), F32)
            dv[h, at, :] = jnp.zeros((tok, HEAD_DIM), F32)
        return carry

    lax.fori_loop(0, members, masks, 0)
    if head == 0:
        hand.start()

    per = QUERY_TILE // tok
    step = KEY_STEP // tok

    def window(i):
        first, last = jnp.int32(0), jnp.int32(tokens)
        for c in range(clips):
            first = jnp.where(ends[c] <= i * QUERY_TILE, ends[c], first)
        for c in reversed(range(clips)):
            last = jnp.where(ends[c] >= (i + 1) * QUERY_TILE, ends[c], last)
        low = first // tok
        return low, (last - low * tok + KEY_STEP - 1) // KEY_STEP

    def block(a, start, number):
        return x_ref[pl.ds(start, number), a * tok : (a + 1) * tok, :].reshape(number * tok, HEAD_DIM)

    def pair(i, carry):
        tiles = (2 * i, 2 * i + 1)
        windows = [window(t) for t in tiles]
        count = jnp.maximum(windows[0][1], windows[1][1])
        q_at = [pl.ds(pl.multiple_of(t * QUERY_TILE, QUERY_TILE), QUERY_TILE) for t in tiles]

        def whole(number):
            both = range(2)
            k0 = [[jnp.minimum(windows[t][0], members - number * step) + j * step for j in range(number)] for t in both]
            k_at = [[pl.ds(pl.multiple_of(k * tok, tok), KEY_STEP) for k in k0[t]] for t in both]
            s, highest = {}, {}
            for j in range(number):
                for t in both:
                    keys = jnp.concatenate([block(1, k0[t][j], step), keymask[k_at[t][j], :]], axis=1)
                    s[t, j] = dot(keys, qt[0, :, q_at[t]], ((1,), (0,)))
                    m = jnp.max(s[t, j].reshape(KEY_STEP // 8, 8, QUERY_TILE), axis=0)
                    highest[t] = m if j == 0 else jnp.maximum(highest[t], m)
            e, total, out = {}, {}, {}
            for t in both:
                top = jnp.max(highest[t], axis=0, keepdims=True)
                for j in range(number):
                    e[t, j] = jnp.exp2((s[t, j] - top) * factor)
                    n = jnp.sum(e[t, j].reshape(KEY_STEP // 8, 8, QUERY_TILE), axis=0)
                    o = dot(vt[0, :, k_at[t][j]], e[t, j].astype(BF16), ((1,), (0,)))
                    total[t] = n if j == 0 else total[t] + n
                    out[t] = o if j == 0 else out[t] + o
            for t in both:
                rows = pl.ds(tiles[t] * per, per)
                inv = 1.0 / jnp.sum(total[t], axis=0, keepdims=True)
                attended = (out[t] * inv).astype(BF16)
                delta = jnp.sum(attended.astype(F32) * gt[0, :, q_at[t]].astype(F32), axis=0, keepdims=True)
                out_ref[rows, :tok, :] = attended.T.reshape(per, tok, HEAD_DIM)
                query, cot = block(0, tiles[t] * per, per), block(3, tiles[t] * per, per)
                for j in range(number):
                    prob = e[t, j] * inv
                    dprob = dot(block(2, k0[t][j], step), gt[0, :, q_at[t]], ((1,), (0,)))
                    dscore = (prob * (dprob - delta)).astype(BF16)
                    dv[0, k_at[t][j], :] += dot(prob.astype(BF16), cot, ((1,), (0,)))
                    dk[0, k_at[t][j], :] += dot(dscore, query, ((1,), (0,)))
                    d = dot(kt[0, :, k_at[t][j]], dscore, ((1,), (0,)))
                    dq = d if j == 0 else dq + d
                out_ref[rows, tok : 2 * tok, :] = (dq * scale).astype(BF16).T.reshape(per, tok, HEAD_DIM)

        for number in range(1, tokens // KEY_STEP + 1):

            @pl.when(count == number)
            def _():
                whole(number)

        return carry

    lax.fori_loop(0, tokens // QUERY_TILE // 2, pair, 0)

    hand.wait()

    def write(n):
        some = pl.ds(n * group, group)
        return pltpu.make_async_copy(out_ref.at[some], out_hbm.at[some, :SLAB, :], out_sem.at[n])

    def finish(i, sums):
        at = pl.ds(pl.multiple_of(i * tok, tok), tok)
        cosine, sine = angles[at, :HEAD_DIM], angles[at, HEAD_DIM:]
        new = []
        for h in range(local):
            dk_tile = (dk[h, at, :] * scale).astype(BF16)
            out_ref[i, h * SLAB + 2 * tok : h * SLAB + 3 * tok, :] = dk_tile
            out_ref[i, h * SLAB + 3 * tok : h * SLAB + 4 * tok, :] = dv[h, at, :].astype(BF16)

        @pl.when(lax.rem(i, group) == group - 1)
        def _():
            write(i // group).start()

        for h in range(local):
            for a, row in ((0, 1), (1, 2)):
                g = out_ref[i, h * SLAB + row * tok : h * SLAB + (row + 1) * tok, :].astype(F32)
                p = x_ref[i, h * SLAB + a * tok : h * SLAB + (a + 1) * tok, :].astype(F32)
                straight = g * p
                across = straight * cosine + g * pltpu.roll(p, HALF, 1) * sine
                plain, turned = sums[2 * h + a]
                new.append(
                    (
                        plain + jnp.sum(straight.reshape(tok // 8, 8, HEAD_DIM), axis=0),
                        turned + jnp.sum(across.reshape(tok // 8, 8, HEAD_DIM), axis=0),
                    )
                )
        return tuple(new)

    zero = jnp.zeros((8, HEAD_DIM), F32)
    sums = lax.fori_loop(0, members, finish, ((zero, zero),) * (2 * local))
    fill = [jnp.zeros((8 - 2, HEAD_DIM), F32)]
    plain, turned = (
        jnp.concatenate([jnp.sum(s[n], axis=0, keepdims=True) for s in sums] + fill, axis=0) for n in range(2)
    )
    plain = plain + pltpu.roll(plain, HALF, 1)
    turned = turned + pltpu.roll(turned, HALF, 1)
    lower = lax.broadcasted_iota(jnp.int32, plain.shape, 1) < HALF
    sums = 0.5 * (plain + jnp.where(lower, turned, -turned))
    if head > 0:
        sums = jnp.concatenate([before_ref[: 2 * head], sums[: 8 - 2 * head]], axis=0)
    sum_ref[...] = sums
    for n in range(members // group):
        write(n).wait()


def insert_kernel(sum_ref, y_hbm, out_hbm, rows_ref, sem):
    del y_hbm
    rest = sum_ref[:4]
    terms = []
    for _ in range(3):
        terms.append(rest.astype(BF16).astype(F32))
        rest = rest - terms[-1]
    rows_ref[...] = jnp.concatenate(terms + [jnp.zeros_like(rest)], axis=0).astype(BF16)
    number = rows_ref.shape[0]
    copies = [
        pltpu.make_async_copy(rows_ref, out_hbm.at[i, SLAB : SLAB + number, :], sem.at[i])
        for i in range(out_hbm.shape[0])
    ]
    for copy in copies:
        copy.start()
    for copy in copies:
        copy.wait()


def spread_copies(j, head, local, y_ref, att_hbm, gv_hbm, sem):
    tokens = att_hbm.shape[0]
    at = slice((j * local + head) * HEAD_DIM, (j * local + head + 1) * HEAD_DIM)
    return [
        pltpu.make_async_copy(y_ref.at[j, row * tokens : (row + 1) * tokens, :], ref.at[:, at], sem.at[j, a])
        for a, (ref, row) in enumerate(((att_hbm, 0), (gv_hbm, 3)))
    ]


def spread_kernel(head, local, y_ref, att_hbm, gv_hbm, sem):
    copies = []
    for j in range(y_ref.shape[0]):
        copies += spread_copies(j, head, local, y_ref, att_hbm, gv_hbm, sem)
    for copy in copies:
        copy.start()
    for copy in copies:
        copy.wait()


def receive_kernel(buckets, ya_hbm, yb_hbm, q_hbm, k_hbm, qg_hbm, kg_hbm, aside_hbm, att_in, gv_in, gq_hbm, gk_hbm, gqg_ref, gkg_ref, att_hbm, gv_hbm, ya, yb, raw, gains, aside, lift_ref, stage, small_sem, raw_sem, y_sem, spread_sem, sem):
    del att_in, gv_in
    tokens, feature = q_hbm.shape
    members = ya_hbm.shape[0]
    local = feature // members // HEAD_DIM
    groups = y_sem.shape[1]
    group = members // groups
    small = [
        pltpu.make_async_copy(source, target, small_sem.at[a])
        for a, (source, target) in enumerate(((qg_hbm, gains.at[0]), (kg_hbm, gains.at[1]), (aside_hbm, aside)))
    ]
    raws = [pltpu.make_async_copy(ref, raw.at[a], raw_sem.at[a]) for a, ref in enumerate((q_hbm, k_hbm))]

    def arrive(n):
        some = slice(n * group, (n + 1) * group)
        return [
            pltpu.make_async_copy(ya_hbm.at[some, tokens : 3 * tokens, :], ya.at[some], y_sem.at[0, n]),
            pltpu.make_async_copy(yb_hbm.at[some], yb.at[some], y_sem.at[1, n]),
        ]

    for copy in small + raws[:1]:
        copy.start()
    for n in range(groups):
        for copy in arrive(n):
            copy.start()
    raws[1].start()
    for copy in small:
        copy.wait()
    copies = []
    parts = sem.shape[1]
    width = feature // parts
    number = 2 * local
    for a, grad_hbm in enumerate((gq_hbm, gk_hbm)):
        raws[a].wait()
        total = jnp.zeros((tokens, HEAD_DIM), F32)
        for j in range(members):
            if a == 0 and j % group == 0:
                for copy in arrive(j // group):
                    copy.wait()
                for n in range(j, j + group):
                    spread = spread_copies(n, 1, local, yb, att_hbm, gv_hbm, spread_sem)
                    for copy in spread:
                        copy.start()
                    copies += spread
            for h, (y_ref, skip) in enumerate(((ya, 0), (yb, tokens))):
                at = slice((j * local + h) * HEAD_DIM, (j * local + h + 1) * HEAD_DIM)
                g = y_ref[j, skip + a * tokens : skip + (a + 1) * tokens, :].astype(F32)
                g = g * aside[0] - pltpu.roll(g, HALF, 1) * aside[1]
                lift = g * gains[a, :, at]
                lift_ref[a, :, at] = lift
                total = total + lift * (raw[a, :, at].astype(F32) * aside[2 + a])
        inner = jnp.sum(total, axis=-1, keepdims=True) / feature
        for part in range(parts):
            for block in range(part * width // HEAD_DIM, (part + 1) * width // HEAD_DIM):
                at = slice(block * HEAD_DIM, (block + 1) * HEAD_DIM)
                hat = raw[a, :, at].astype(F32) * aside[2 + a]
                stage[a, :, at] = (aside[2 + a] * (lift_ref[a, :, at] - hat * inner)).astype(BF16)
            at = slice(part * width, (part + 1) * width)
            copies.append(pltpu.make_async_copy(stage.at[a, :, at], grad_hbm.at[:, at], sem.at[a, part]))
            copies[-1].start()
    for j in range(members):
        rows = yb[j, SLAB:, :].astype(F32)
        total = rows[:number] + rows[number : 2 * number] + rows[2 * number : 3 * number]
        for h in range(local):
            at = slice((j * local + h) * HEAD_DIM, (j * local + h + 1) * HEAD_DIM)
            gqg_ref[:, at] = total[2 * h : 2 * h + 1] / (gains[0, :, at] * buckets)
            gkg_ref[:, at] = total[2 * h + 1 : 2 * h + 2] / (gains[1, :, at] * buckets)
    for copy in copies:
        copy.wait()


def on_device(q_raw, k_raw, values, grad_out, q_gain, k_gain, lengths, positions):
    members = lax.axis_size("seq")
    replicas = lax.axis_size("dp")
    _, tok, feature = q_raw.shape
    local = feature // members // HEAD_DIM
    tokens = tok * members
    vmem = pl.BlockSpec(memory_space=pltpu.VMEM)
    smem = pl.BlockSpec(memory_space=pltpu.SMEM)
    hbm = pl.BlockSpec(memory_space=pltpu.HBM)
    sems = pltpu.SemaphoreType.DMA
    table = jnp.asarray(rotary_table())
    doubled = jnp.asarray(double_table())
    shape = jax.ShapeDtypeStruct
    slabs = shape((members, SLAB, HEAD_DIM), BF16)
    longer = shape((members, SLAB + 16, HEAD_DIM), BF16)
    row_shape = shape((tok, feature), BF16)

    def send(head, aside):
        first = head == 0
        packet = longer if first else slabs
        scratch = [pltpu.VMEM((4, tok, feature), BF16), pltpu.VMEM((2, 1, feature), F32)]
        if first:
            scratch += [pltpu.VMEM((3, 1, tok), jnp.int32), pltpu.VMEM(table.shape, BF16)]
        return pl.pallas_call(
            functools.partial(send_kernel, head),
            out_shape=(packet, shape((4, tok, HEAD_DIM), F32)) if first else packet,
            in_specs=[hbm] * 8 + ([] if first else [vmem]),
            out_specs=(hbm, vmem) if first else hbm,
            scratch_shapes=scratch + [pltpu.VMEM(packet.shape, BF16), sems((4,)), sems((4,)), sems((4,))],
            compiler_params=pltpu.CompilerParams(vmem_limit_bytes=60 << 20),
            cost_estimate=pl.CostEstimate(flops=20 << 20, bytes_accessed=6 << 20, transcendentals=0),
            name="send",
        )(
            *(a[0] for a in (q_raw, k_raw, values, grad_out)),
            q_gain[None],
            k_gain[None],
            jnp.transpose(positions, (1, 0, 2)),
            table,
            *([] if first else [aside]),
        )

    def exchange(packet):
        return lax.all_to_all(packet, "seq", 0, 0, tiled=True)

    angle_shape = shape((tokens, 2 * HEAD_DIM), F32)

    def attend(head, got, *others):
        first = head == 0
        outs = (longer if head == local - 1 else slabs, shape((8, HEAD_DIM), F32))
        return pl.pallas_call(
            functools.partial(attention_kernel, head),
            out_shape=outs + ((angle_shape,) if first else ()),
            in_specs=[smem, hbm] + ([vmem] if first else [hbm, vmem]),
            out_specs=(hbm, vmem) + ((hbm,) if first else ()),
            scratch_shapes=[
                pltpu.VMEM(got.shape, BF16),
                pltpu.VMEM((members, SLAB, HEAD_DIM), BF16),
                pltpu.VMEM((1, 2 * HEAD_DIM, tokens), BF16),
                pltpu.VMEM((1, HEAD_DIM, tokens), BF16),
                pltpu.VMEM((1, HEAD_DIM, tokens), BF16),
                pltpu.VMEM((1, HEAD_DIM, tokens), BF16),
                pltpu.VMEM((tokens, HEAD_DIM), BF16),
                pltpu.VMEM((1, tokens, HEAD_DIM), F32),
                pltpu.VMEM((1, tokens, HEAD_DIM), F32),
                pltpu.VMEM(angle_shape.shape, F32),
                sems((4,)),
                sems((4,)),
                sems(()),
            ],
            compiler_params=pltpu.CompilerParams(vmem_limit_bytes=60 << 20),
            cost_estimate=pl.CostEstimate(flops=10 << 30, bytes_accessed=5 << 20, transcendentals=1 << 22),
            name="attention",
        )(lengths[0], got, *others)

    packet_a, aside = send(0, None)
    got_a = exchange(packet_a)
    packet_b = send(1, aside)
    got_b = exchange(packet_b)
    back_a, sum_a, angles = attend(0, got_a, doubled)
    y_a = exchange(back_a)
    back_b, sums = attend(1, got_b, angles, sum_a)
    for distance in (1, 2, 4):
        sums = sums + lax.ppermute(sums, "dp", [(i, i ^ distance) for i in range(replicas)])
    back_b = pl.pallas_call(
        insert_kernel,
        out_shape=longer,
        in_specs=[vmem, hbm],
        out_specs=hbm,
        scratch_shapes=[pltpu.VMEM((16, HEAD_DIM), BF16), sems((members,))],
        input_output_aliases={1: 0},
        name="insert",
    )(sums, back_b)
    y_b = exchange(back_b)
    attended, grad_v = pl.pallas_call(
        functools.partial(spread_kernel, 0, local),
        out_shape=(row_shape,) * 2,
        in_specs=[vmem],
        out_specs=(hbm, hbm),
        scratch_shapes=[sems((members, 2))],
        compiler_params=pltpu.CompilerParams(vmem_limit_bytes=24 << 20),
        cost_estimate=pl.CostEstimate(flops=0, bytes_accessed=4 << 20, transcendentals=0),
        name="receive_spread",
    )(y_a)
    grad_q, grad_k, q_sum, k_sum, attended, grad_v = pl.pallas_call(
        functools.partial(receive_kernel, replicas),
        out_shape=(row_shape, row_shape, shape((1, feature), F32), shape((1, feature), F32), row_shape, row_shape),
        in_specs=[hbm] * 9,
        out_specs=(hbm, hbm, vmem, vmem, hbm, hbm),
        scratch_shapes=[
            pltpu.VMEM((members, 2 * tok, HEAD_DIM), BF16),
            pltpu.VMEM(longer.shape, BF16),
            pltpu.VMEM((2, tok, feature), BF16),
            pltpu.VMEM((2, 1, feature), F32),
            pltpu.VMEM((4, tok, HEAD_DIM), F32),
            pltpu.VMEM((2, tok, feature), F32),
            pltpu.VMEM((2, tok, feature), BF16),
            sems((3,)),
            sems((2,)),
            sems((2, 4)),
            sems((members, 2)),
            sems((2, 4)),
        ],
        input_output_aliases={7: 4, 8: 5},
        compiler_params=pltpu.CompilerParams(vmem_limit_bytes=60 << 20),
        cost_estimate=pl.CostEstimate(flops=40 << 20, bytes_accessed=8 << 20, transcendentals=0),
        name="receive",
    )(y_a, y_b, q_raw[0], k_raw[0], q_gain[None], k_gain[None], aside, attended, grad_v)
    return tuple(o[None] for o in (attended, grad_q, grad_k, grad_v)) + (q_sum[0], k_sum[0])


def solution(mesh):
    tokens_split = P("dp", "seq", None)
    return jax.shard_map(
        on_device,
        mesh=mesh,
        in_specs=(tokens_split,) * 4 + (P(), P(), P("dp", None), P("dp", None, "seq")),
        out_specs=(tokens_split,) * 4 + (P(), P()),
        check_vma=False,
    )
```

```python
import functools
import math

import jax
import jax.numpy as jnp
import numpy as np
from jax import lax
from jax.experimental import pallas as pl
from jax.experimental.pallas import tpu as pltpu
from jax.sharding import PartitionSpec as P

HEAD_DIM = 128
HALF = HEAD_DIM // 2
EPSILON = 1e-06
APART = float(2**20)
QUERY_TILE = 256
KEY_STEP = 512
SLAB = 4 * HEAD_DIM
F32 = jnp.float32
BF16 = jnp.bfloat16


GRID = 64


def rotary_table():
    sixth = HEAD_DIM // 6
    first = HALF - 2 * sixth
    table = np.zeros((3, GRID, HEAD_DIM))
    begin = 0
    for section, count in enumerate((first, sixth, sixth)):
        freqs = 10000.0 ** (-np.arange(count) / count)
        angle = np.arange(GRID)[:, None] * freqs[None]
        table[section, :, begin : begin + count] = np.cos(angle)
        table[section, :, HALF + begin : HALF + begin + count] = np.sin(angle)
        begin += count
    rest = table.reshape(3 * GRID, HEAD_DIM)
    terms = []
    for _ in range(3):
        terms.append(rest.astype(np.float32).astype(jnp.bfloat16))
        rest = rest - terms[-1].astype(np.float64)
    return np.concatenate(terms, axis=1)


def dot(left, right, contract):
    return lax.dot_general(left, right, ((contract[0], contract[1]), ((), ())), preferred_element_type=F32)


def rotary(rows, table):
    tokens = rows[0].shape[1]
    terms = dot(picks_of(rows), table, ((0,), (0,)))
    both = terms[:, :HEAD_DIM] + terms[:, HEAD_DIM : 2 * HEAD_DIM] + terms[:, 2 * HEAD_DIM :]
    other = pltpu.roll(both, HALF, 1)
    lower = lax.broadcasted_iota(jnp.int32, (tokens, HEAD_DIM), 1) < HALF
    return jnp.where(lower, both, other), jnp.where(lower, -other, both)


def double_table():
    sixth = HEAD_DIM // 6
    first = HALF - 2 * sixth
    table = np.zeros((3, GRID, 2, 2, HALF))
    begin = 0
    for section, count in enumerate((first, sixth, sixth)):
        angle = 2 * np.arange(GRID)[:, None] * 10000.0 ** (-np.arange(count) / count)[None]
        at = slice(begin, begin + count)
        table[section, :, 0, 0, at], table[section, :, 0, 1, at] = np.cos(angle), -np.cos(angle)
        table[section, :, 1, 0, at] = table[section, :, 1, 1, at] = np.sin(angle)
        begin += count
    table = table.reshape(3 * GRID, 2 * HEAD_DIM)
    high = table.astype(np.float32).astype(jnp.bfloat16)
    return np.concatenate([high, (table - high.astype(np.float64)).astype(np.float32).astype(jnp.bfloat16)], axis=1)


def picks_of(rows):
    number = lax.broadcasted_iota(jnp.int32, (GRID, rows[0].shape[1]), 0).astype(F32)
    return jnp.concatenate([jnp.where(number == row, 1.0, 0.0) for row in rows], axis=0).astype(BF16)


def columns(block):
    return pl.ds(pl.multiple_of(block * HEAD_DIM, HEAD_DIM), HEAD_DIM)


def send_kernel(head, q_hbm, k_hbm, v_hbm, g_hbm, qg_hbm, kg_hbm, pos_hbm, table_hbm, *rest):
    if head == 0:
        out_hbm, aside_ref, raw, gains, pos_ref, table_ref, stage, in_sem, small_sem, out_sem = rest
    else:
        aside_ref, out_hbm, raw, gains, stage, in_sem, small_sem, out_sem = rest
    tokens, feature = q_hbm.shape
    members = out_hbm.shape[0]
    local = feature // members // HEAD_DIM
    sources = [(qg_hbm, gains.at[0]), (kg_hbm, gains.at[1])]
    if head == 0:
        sources += [(pos_hbm, pos_ref), (table_hbm, table_ref)]
    small = [pltpu.make_async_copy(source, target, small_sem.at[a]) for a, (source, target) in enumerate(sources)]
    reads = [pltpu.make_async_copy(ref, raw.at[a], in_sem.at[a]) for a, ref in enumerate((q_hbm, k_hbm, v_hbm, g_hbm))]
    for copy in small + reads:
        copy.start()
    for copy in small:
        copy.wait()
    if head == 0:
        rows = [pos_ref[a].astype(F32) for a in range(3)]
        aside_ref[0], aside_ref[1] = rotary(rows, table_ref[...])
        place = jnp.concatenate(rows + [jnp.zeros((13, tokens), F32)], axis=0).astype(BF16)
    for a in range(2):
        reads[a].wait()
        if head == 0:
            total = jnp.zeros((tokens, HEAD_DIM), F32)
            for h in range(feature // HEAD_DIM):
                part = raw[a, :, h * HEAD_DIM : (h + 1) * HEAD_DIM].astype(F32)
                total = total + part * part
            scale = lax.rsqrt(jnp.sum(total, axis=-1, keepdims=True) / feature + EPSILON)
            aside_ref[2 + a] = jnp.broadcast_to(scale, (tokens, HEAD_DIM))
    reads[2].wait()
    reads[3].wait()
    packets = []
    group = members // out_sem.shape[0]
    for j in range(members):
        at = slice((j * local + head) * HEAD_DIM, (j * local + head + 1) * HEAD_DIM)
        for a in range(2):
            x = raw[a, :, at].astype(F32) * aside_ref[2 + a] * gains[a, :, at]
            turned = x * aside_ref[0] + pltpu.roll(x, HALF, 1) * aside_ref[1]
            stage[j, a * tokens : (a + 1) * tokens, :] = turned.astype(BF16)
        for a in (2, 3):
            stage[j, a * tokens : (a + 1) * tokens, :] = raw[a, :, at]
        if head == 0:
            stage[j, SLAB:, :] = place
        if j % group == group - 1:
            some = slice(j + 1 - group, j + 1)
            packets.append(pltpu.make_async_copy(stage.at[some], out_hbm.at[some], out_sem.at[j // group]))
            packets[-1].start()
    for copy in packets:
        copy.wait()


def attention_kernel(head, len_ref, x_ref, *rest):
    if head == 0:
        table_ref, out_hbm, sum_ref, angles_hbm, *rest = rest
    else:
        angles_hbm, before_ref, out_hbm, sum_ref, *rest = rest
    out_ref, qt, kt, vt, gt, keymask, dk, dv, angles, out_sem, angle_sem = rest
    members = x_ref.shape[0]
    tok = HEAD_DIM
    tokens = members * tok
    local = 1
    clips = len_ref.shape[0]
    scale = HEAD_DIM ** (-0.5)
    factor = scale * math.log2(math.e)

    group = members // out_sem.shape[0]
    if head == 0:
        hand = pltpu.make_async_copy(angles, angles_hbm, angle_sem)
    else:
        hand = pltpu.make_async_copy(angles_hbm, angles, angle_sem)
        hand.start()
    ends = []
    so_far = 0
    for c in range(clips):
        so_far = so_far + len_ref[c]
        ends.append(so_far)

    def masks(i, carry):
        token = lax.broadcasted_iota(jnp.int32, (tok, HEAD_DIM), 0) + i * tok
        lane = lax.broadcasted_iota(jnp.int32, (tok, HEAD_DIM), 1)
        clip = jnp.zeros((tok, HEAD_DIM), jnp.int32)
        for c in range(clips):
            clip = clip + (token >= ends[c]).astype(jnp.int32)
        own = clip == lane
        at = pl.ds(pl.multiple_of(i * tok, tok), tok)
        keymask[at, :] = jnp.where(own, -APART, 0.0).astype(BF16)
        token = lax.broadcasted_iota(jnp.int32, (HEAD_DIM, tok), 1) + i * tok
        lane = lax.broadcasted_iota(jnp.int32, (HEAD_DIM, tok), 0)
        clip = jnp.zeros((HEAD_DIM, tok), jnp.int32)
        for c in range(clips):
            clip = clip + (token >= ends[c]).astype(jnp.int32)
        apart = jnp.where(clip == lane, 0.0, 1.0).astype(BF16)
        if head == 0:
            rows = x_ref[i, SLAB:, :].astype(F32)
            terms = dot(picks_of([rows[a : a + 1] for a in range(3)]), table_ref[...], ((0,), (0,)))
            angles[at, :] = terms[:, : 2 * HEAD_DIM] + terms[:, 2 * HEAD_DIM :]
        for h in range(local):
            qt[h, :HEAD_DIM, at] = x_ref[i, h * SLAB : h * SLAB + tok, :].T
            qt[h, HEAD_DIM:, at] = apart
            gt[h, :, at] = x_ref[i, h * SLAB + 3 * tok : h * SLAB + 4 * tok, :].T
            kt[h, :, at] = x_ref[i, h * SLAB + tok : h * SLAB + 2 * tok, :].T
            vt[h, :, at] = x_ref[i, h * SLAB + 2 * tok : h * SLAB + 3 * tok, :].T
            dk[h, at, :] = jnp.zeros((tok, HEAD_DIM), F32)
            dv[h, at, :] = jnp.zeros((tok, HEAD_DIM), F32)
        return carry

    lax.fori_loop(0, members, masks, 0)
    if head == 0:
        hand.start()

    per = QUERY_TILE // tok
    step = KEY_STEP // tok

    def window(i):
        first, last = jnp.int32(0), jnp.int32(tokens)
        for c in range(clips):
            first = jnp.where(ends[c] <= i * QUERY_TILE, ends[c], first)
        for c in reversed(range(clips)):
            last = jnp.where(ends[c] >= (i + 1) * QUERY_TILE, ends[c], last)
        low = first // tok
        return low, (last - low * tok + KEY_STEP - 1) // KEY_STEP

    def block(a, start, number):
        return x_ref[pl.ds(start, number), a * tok : (a + 1) * tok, :].reshape(number * tok, HEAD_DIM)

    def pair(i, carry):
        tiles = (2 * i, 2 * i + 1)
        windows = [window(t) for t in tiles]
        count = jnp.maximum(windows[0][1], windows[1][1])
        q_at = [pl.ds(pl.multiple_of(t * QUERY_TILE, QUERY_TILE), QUERY_TILE) for t in tiles]

        def whole(number):
            both = range(2)
            k0 = [[jnp.minimum(windows[t][0], members - number * step) + j * step for j in range(number)] for t in both]
            k_at = [[pl.ds(pl.multiple_of(k * tok, tok), KEY_STEP) for k in k0[t]] for t in both]
            s, highest = {}, {}
            for j in range(number):
                for t in both:
                    keys = jnp.concatenate([block(1, k0[t][j], step), keymask[k_at[t][j], :]], axis=1)
                    s[t, j] = dot(keys, qt[0, :, q_at[t]], ((1,), (0,)))
                    m = jnp.max(s[t, j].reshape(KEY_STEP // 8, 8, QUERY_TILE), axis=0)
                    highest[t] = m if j == 0 else jnp.maximum(highest[t], m)
            e, total, out = {}, {}, {}
            for t in both:
                top = jnp.max(highest[t], axis=0, keepdims=True)
                for j in range(number):
                    e[t, j] = jnp.exp2((s[t, j] - top) * factor)
                    n = jnp.sum(e[t, j].reshape(KEY_STEP // 8, 8, QUERY_TILE), axis=0)
                    o = dot(vt[0, :, k_at[t][j]], e[t, j].astype(BF16), ((1,), (0,)))
                    total[t] = n if j == 0 else total[t] + n
                    out[t] = o if j == 0 else out[t] + o
            for t in both:
                rows = pl.ds(tiles[t] * per, per)
                inv = 1.0 / jnp.sum(total[t], axis=0, keepdims=True)
                attended = (out[t] * inv).astype(BF16)
                delta = jnp.sum(attended.astype(F32) * gt[0, :, q_at[t]].astype(F32), axis=0, keepdims=True)
                out_ref[rows, :tok, :] = attended.T.reshape(per, tok, HEAD_DIM)
                query, cot = block(0, tiles[t] * per, per), block(3, tiles[t] * per, per)
                for j in range(number):
                    prob = e[t, j] * inv
                    dprob = dot(block(2, k0[t][j], step), gt[0, :, q_at[t]], ((1,), (0,)))
                    dscore = (prob * (dprob - delta)).astype(BF16)
                    dv[0, k_at[t][j], :] += dot(prob.astype(BF16), cot, ((1,), (0,)))
                    dk[0, k_at[t][j], :] += dot(dscore, query, ((1,), (0,)))
                    d = dot(kt[0, :, k_at[t][j]], dscore, ((1,), (0,)))
                    dq = d if j == 0 else dq + d
                out_ref[rows, tok : 2 * tok, :] = (dq * scale).astype(BF16).T.reshape(per, tok, HEAD_DIM)

        for number in range(1, tokens // KEY_STEP + 1):

            @pl.when(count == number)
            def _():
                whole(number)

        return carry

    lax.fori_loop(0, tokens // QUERY_TILE // 2, pair, 0)

    hand.wait()

    def write(n):
        some = pl.ds(n * group, group)
        return pltpu.make_async_copy(out_ref.at[some], out_hbm.at[some, :SLAB, :], out_sem.at[n])

    def finish(i, sums):
        at = pl.ds(pl.multiple_of(i * tok, tok), tok)
        cosine, sine = angles[at, :HEAD_DIM], angles[at, HEAD_DIM:]
        new = []
        for h in range(local):
            dk_tile = (dk[h, at, :] * scale).astype(BF16)
            out_ref[i, h * SLAB + 2 * tok : h * SLAB + 3 * tok, :] = dk_tile
            out_ref[i, h * SLAB + 3 * tok : h * SLAB + 4 * tok, :] = dv[h, at, :].astype(BF16)

        @pl.when(lax.rem(i, group) == group - 1)
        def _():
            write(i // group).start()

        for h in range(local):
            for a, row in ((0, 1), (1, 2)):
                g = out_ref[i, h * SLAB + row * tok : h * SLAB + (row + 1) * tok, :].astype(F32)
                p = x_ref[i, h * SLAB + a * tok : h * SLAB + (a + 1) * tok, :].astype(F32)
                straight = g * p
                across = straight * cosine + g * pltpu.roll(p, HALF, 1) * sine
                plain, turned = sums[2 * h + a]
                new.append(
                    (
                        plain + jnp.sum(straight.reshape(tok // 8, 8, HEAD_DIM), axis=0),
                        turned + jnp.sum(across.reshape(tok // 8, 8, HEAD_DIM), axis=0),
                    )
                )
        return tuple(new)

    zero = jnp.zeros((8, HEAD_DIM), F32)
    sums = lax.fori_loop(0, members, finish, ((zero, zero),) * (2 * local))
    fill = [jnp.zeros((8 - 2, HEAD_DIM), F32)]
    plain, turned = (
        jnp.concatenate([jnp.sum(s[n], axis=0, keepdims=True) for s in sums] + fill, axis=0) for n in range(2)
    )
    plain = plain + pltpu.roll(plain, HALF, 1)
    turned = turned + pltpu.roll(turned, HALF, 1)
    lower = lax.broadcasted_iota(jnp.int32, plain.shape, 1) < HALF
    sums = 0.5 * (plain + jnp.where(lower, turned, -turned))
    if head > 0:
        sums = jnp.concatenate([before_ref[: 2 * head], sums[: 8 - 2 * head]], axis=0)
    sum_ref[...] = sums
    for n in range(members // group):
        write(n).wait()


def insert_kernel(sum_ref, y_hbm, out_hbm, rows_ref, sem):
    del y_hbm
    rest = sum_ref[:4]
    terms = []
    for _ in range(3):
        terms.append(rest.astype(BF16).astype(F32))
        rest = rest - terms[-1]
    rows_ref[...] = jnp.concatenate(terms + [jnp.zeros_like(rest)], axis=0).astype(BF16)
    number = rows_ref.shape[0]
    copies = [
        pltpu.make_async_copy(rows_ref, out_hbm.at[i, SLAB : SLAB + number, :], sem.at[i])
        for i in range(out_hbm.shape[0])
    ]
    for copy in copies:
        copy.start()
    for copy in copies:
        copy.wait()


def spread_copies(j, head, local, y_ref, att_hbm, gv_hbm, sem):
    tokens = att_hbm.shape[0]
    at = slice((j * local + head) * HEAD_DIM, (j * local + head + 1) * HEAD_DIM)
    return [
        pltpu.make_async_copy(y_ref.at[j, row * tokens : (row + 1) * tokens, :], ref.at[:, at], sem.at[j, a])
        for a, (ref, row) in enumerate(((att_hbm, 0), (gv_hbm, 3)))
    ]


def early_kernel(local, y_ref, q_ref, k_ref, qg_ref, kg_ref, aside_ref, att_hbm, gv_hbm, lift_hbm, total_ref, lift_ref, spread_sem, lift_sem):
    tokens = q_ref.shape[0]
    members = y_ref.shape[0]
    copies = []
    for j in range(members):
        copies += spread_copies(j, 0, local, y_ref, att_hbm, gv_hbm, spread_sem)
    for copy in copies:
        copy.start()
    for a, (raw_ref, gain_ref) in enumerate(((q_ref, qg_ref), (k_ref, kg_ref))):
        total = jnp.zeros((tokens, HEAD_DIM), F32)
        for j in range(members):
            at = slice(j * local * HEAD_DIM, (j * local + 1) * HEAD_DIM)
            g = y_ref[j, (a + 1) * tokens : (a + 2) * tokens, :].astype(F32)
            g = g * aside_ref[0] - pltpu.roll(g, HALF, 1) * aside_ref[1]
            lift = g * gain_ref[:, at]
            lift_ref[a, :, j * HEAD_DIM : (j + 1) * HEAD_DIM] = lift
            total = total + lift * (raw_ref[:, at].astype(F32) * aside_ref[2 + a])
        total_ref[a] = total
        copies.append(pltpu.make_async_copy(lift_ref.at[a], lift_hbm.at[a], lift_sem.at[a]))
        copies[-1].start()
    for copy in copies:
        copy.wait()


def receive_kernel(buckets, yb_hbm, q_hbm, k_hbm, qg_hbm, kg_hbm, aside_hbm, lift_hbm, total_hbm, att_in, gv_in, gq_hbm, gk_hbm, gqg_ref, gkg_ref, att_hbm, gv_hbm, yb, raw, gains, aside, before, totals, lift_ref, stage, small_sem, raw_sem, lift_sem, y_sem, spread_sem, sem):
    del att_in, gv_in
    tokens, feature = q_hbm.shape
    members = yb_hbm.shape[0]
    local = feature // members // HEAD_DIM
    groups = y_sem.shape[0]
    group = members // groups
    sources = ((aside_hbm, aside), (total_hbm, totals), (qg_hbm, gains.at[0]), (kg_hbm, gains.at[1]))
    small = [pltpu.make_async_copy(source, target, small_sem.at[a]) for a, (source, target) in enumerate(sources)]
    raws = [pltpu.make_async_copy(ref, raw.at[a], raw_sem.at[a]) for a, ref in enumerate((q_hbm, k_hbm))]
    lifts = [pltpu.make_async_copy(lift_hbm.at[a], before.at[a], lift_sem.at[a]) for a in range(2)]

    def arrive(n):
        some = slice(n * group, (n + 1) * group)
        return pltpu.make_async_copy(yb_hbm.at[some], yb.at[some], y_sem.at[n])

    for copy in small + raws[:1]:
        copy.start()
    for n in range(groups):
        arrive(n).start()
    for copy in lifts[:1] + raws[1:] + lifts[1:]:
        copy.start()
    for copy in small:
        copy.wait()
    copies = []
    parts = sem.shape[1]
    width = feature // parts
    number = 2 * local
    for a, grad_hbm in enumerate((gq_hbm, gk_hbm)):
        raws[a].wait()
        total = totals[a]
        for j in range(members):
            if a == 0 and j % group == 0:
                arrive(j // group).wait()
                for n in range(j, j + group):
                    spread = spread_copies(n, 1, local, yb, att_hbm, gv_hbm, spread_sem)
                    for copy in spread:
                        copy.start()
                    copies += spread
            at = slice((j * local + 1) * HEAD_DIM, (j * local + 2) * HEAD_DIM)
            g = yb[j, (a + 1) * tokens : (a + 2) * tokens, :].astype(F32)
            g = g * aside[0] - pltpu.roll(g, HALF, 1) * aside[1]
            lift = g * gains[a, :, at]
            lift_ref[a, :, j * HEAD_DIM : (j + 1) * HEAD_DIM] = lift
            total = total + lift * (raw[a, :, at].astype(F32) * aside[2 + a])
        inner = jnp.sum(total, axis=-1, keepdims=True) / feature
        lean = jnp.broadcast_to(inner, (tokens, HEAD_DIM)) * aside[2 + a]
        lifts[a].wait()
        for part in range(parts):
            for block in range(part * width // HEAD_DIM, (part + 1) * width // HEAD_DIM):
                at = slice(block * HEAD_DIM, (block + 1) * HEAD_DIM)
                j, h = divmod(block, local)
                lift = (before, lift_ref)[h][a, :, j * HEAD_DIM : (j + 1) * HEAD_DIM]
                stage[a, :, at] = (aside[2 + a] * (lift - raw[a, :, at].astype(F32) * lean)).astype(BF16)
            at = slice(part * width, (part + 1) * width)
            copies.append(pltpu.make_async_copy(stage.at[a, :, at], grad_hbm.at[:, at], sem.at[a, part]))
            copies[-1].start()
    for j in range(members):
        rows = yb[j, SLAB:, :].astype(F32)
        total = rows[:number] + rows[number : 2 * number] + rows[2 * number : 3 * number]
        for h in range(local):
            at = slice((j * local + h) * HEAD_DIM, (j * local + h + 1) * HEAD_DIM)
            gqg_ref[:, at] = total[2 * h : 2 * h + 1] / (gains[0, :, at] * buckets)
            gkg_ref[:, at] = total[2 * h + 1 : 2 * h + 2] / (gains[1, :, at] * buckets)
    for copy in copies:
        copy.wait()


def on_device(q_raw, k_raw, values, grad_out, q_gain, k_gain, lengths, positions):
    members = lax.axis_size("seq")
    replicas = lax.axis_size("dp")
    _, tok, feature = q_raw.shape
    local = feature // members // HEAD_DIM
    tokens = tok * members
    vmem = pl.BlockSpec(memory_space=pltpu.VMEM)
    smem = pl.BlockSpec(memory_space=pltpu.SMEM)
    hbm = pl.BlockSpec(memory_space=pltpu.HBM)
    sems = pltpu.SemaphoreType.DMA
    table = jnp.asarray(rotary_table())
    doubled = jnp.asarray(double_table())
    shape = jax.ShapeDtypeStruct
    slabs = shape((members, SLAB, HEAD_DIM), BF16)
    longer = shape((members, SLAB + 16, HEAD_DIM), BF16)
    row_shape = shape((tok, feature), BF16)

    def send(head, aside):
        first = head == 0
        packet = longer if first else slabs
        scratch = [pltpu.VMEM((4, tok, feature), BF16), pltpu.VMEM((2, 1, feature), F32)]
        if first:
            scratch += [pltpu.VMEM((3, 1, tok), jnp.int32), pltpu.VMEM(table.shape, BF16)]
        return pl.pallas_call(
            functools.partial(send_kernel, head),
            out_shape=(packet, shape((4, tok, HEAD_DIM), F32)) if first else packet,
            in_specs=[hbm] * 8 + ([] if first else [vmem]),
            out_specs=(hbm, vmem) if first else hbm,
            scratch_shapes=scratch + [pltpu.VMEM(packet.shape, BF16), sems((4,)), sems((4,)), sems((4,))],
            compiler_params=pltpu.CompilerParams(vmem_limit_bytes=60 << 20),
            cost_estimate=pl.CostEstimate(flops=20 << 20, bytes_accessed=6 << 20, transcendentals=0),
            name="send",
        )(
            *(a[0] for a in (q_raw, k_raw, values, grad_out)),
            q_gain[None],
            k_gain[None],
            jnp.transpose(positions, (1, 0, 2)),
            table,
            *([] if first else [aside]),
        )

    def exchange(packet):
        return lax.all_to_all(packet, "seq", 0, 0, tiled=True)

    angle_shape = shape((tokens, 2 * HEAD_DIM), F32)

    def attend(head, got, *others):
        first = head == 0
        outs = (longer if head == local - 1 else slabs, shape((8, HEAD_DIM), F32))
        return pl.pallas_call(
            functools.partial(attention_kernel, head),
            out_shape=outs + ((angle_shape,) if first else ()),
            in_specs=[smem, vmem] + ([vmem] if first else [hbm, vmem]),
            out_specs=(hbm, vmem) + ((hbm,) if first else ()),
            scratch_shapes=[
                pltpu.VMEM((members, SLAB, HEAD_DIM), BF16),
                pltpu.VMEM((1, 2 * HEAD_DIM, tokens), BF16),
                pltpu.VMEM((1, HEAD_DIM, tokens), BF16),
                pltpu.VMEM((1, HEAD_DIM, tokens), BF16),
                pltpu.VMEM((1, HEAD_DIM, tokens), BF16),
                pltpu.VMEM((tokens, HEAD_DIM), BF16),
                pltpu.VMEM((1, tokens, HEAD_DIM), F32),
                pltpu.VMEM((1, tokens, HEAD_DIM), F32),
                pltpu.VMEM(angle_shape.shape, F32),
                sems((4,)),
                sems(()),
            ],
            compiler_params=pltpu.CompilerParams(vmem_limit_bytes=50 << 20),
            cost_estimate=pl.CostEstimate(flops=10 << 30, bytes_accessed=5 << 20, transcendentals=1 << 22),
            name="attention",
        )(lengths[0], got, *others)

    packet_a, aside = send(0, None)
    got_a = exchange(packet_a)
    packet_b = send(1, aside)
    got_b = exchange(packet_b)
    back_a, sum_a, angles = attend(0, got_a, doubled)
    y_a = exchange(back_a)
    back_b, sums = attend(1, got_b, angles, sum_a)
    for distance in (1, 2, 4):
        sums = sums + lax.ppermute(sums, "dp", [(i, i ^ distance) for i in range(replicas)])
    back_b = pl.pallas_call(
        insert_kernel,
        out_shape=longer,
        in_specs=[vmem, hbm],
        out_specs=hbm,
        scratch_shapes=[pltpu.VMEM((16, HEAD_DIM), BF16), sems((members,))],
        input_output_aliases={1: 0},
        name="insert",
    )(sums, back_b)
    y_b = exchange(back_b)
    half_shape = shape((2, tok, feature // local), F32)
    total_shape = shape((2, tok, HEAD_DIM), F32)
    attended, grad_v, lift, totals = pl.pallas_call(
        functools.partial(early_kernel, local),
        out_shape=(row_shape, row_shape, half_shape, total_shape),
        in_specs=[vmem] * 6,
        out_specs=(hbm, hbm, hbm, vmem),
        scratch_shapes=[pltpu.VMEM(half_shape.shape, F32), sems((members, 2)), sems((2,))],
        compiler_params=pltpu.CompilerParams(vmem_limit_bytes=24 << 20),
        cost_estimate=pl.CostEstimate(flops=20 << 20, bytes_accessed=6 << 20, transcendentals=0),
        name="early",
    )(y_a, q_raw[0], k_raw[0], q_gain[None], k_gain[None], aside)
    grad_q, grad_k, q_sum, k_sum, attended, grad_v = pl.pallas_call(
        functools.partial(receive_kernel, replicas),
        out_shape=(row_shape, row_shape, shape((1, feature), F32), shape((1, feature), F32), row_shape, row_shape),
        in_specs=[hbm] * 10,
        out_specs=(hbm, hbm, vmem, vmem, hbm, hbm),
        scratch_shapes=[
            pltpu.VMEM(longer.shape, BF16),
            pltpu.VMEM((2, tok, feature), BF16),
            pltpu.VMEM((2, 1, feature), F32),
            pltpu.VMEM((4, tok, HEAD_DIM), F32),
            pltpu.VMEM(half_shape.shape, F32),
            pltpu.VMEM(total_shape.shape, F32),
            pltpu.VMEM(half_shape.shape, F32),
            pltpu.VMEM((2, tok, feature), BF16),
            sems((4,)),
            sems((2,)),
            sems((2,)),
            sems((4,)),
            sems((members, 2)),
            sems((2, 4)),
        ],
        input_output_aliases={8: 4, 9: 5},
        compiler_params=pltpu.CompilerParams(vmem_limit_bytes=60 << 20),
        cost_estimate=pl.CostEstimate(flops=40 << 20, bytes_accessed=8 << 20, transcendentals=0),
        name="receive",
    )(y_b, q_raw[0], k_raw[0], q_gain[None], k_gain[None], aside, lift, totals, attended, grad_v)
    return tuple(o[None] for o in (attended, grad_q, grad_k, grad_v)) + (q_sum[0], k_sum[0])


def solution(mesh):
    tokens_split = P("dp", "seq", None)
    return jax.shard_map(
        on_device,
        mesh=mesh,
        in_specs=(tokens_split,) * 4 + (P(), P(), P("dp", None), P("dp", None, "seq")),
        out_specs=(tokens_split,) * 4 + (P(), P()),
        check_vma=False,
    )
```

```python
import functools
import math

import jax
import jax.numpy as jnp
import numpy as np
from jax import lax
from jax.experimental import pallas as pl
from jax.experimental.pallas import tpu as pltpu
from jax.sharding import PartitionSpec as P

HEAD_DIM = 128
HALF = HEAD_DIM // 2
EPSILON = 1e-06
APART = float(2**20)
QUERY_TILE = 256
KEY_STEP = 512
SLAB = 4 * HEAD_DIM
F32 = jnp.float32
BF16 = jnp.bfloat16


GRID = 64


def rotary_table():
    sixth = HEAD_DIM // 6
    first = HALF - 2 * sixth
    table = np.zeros((3, GRID, HEAD_DIM))
    begin = 0
    for section, count in enumerate((first, sixth, sixth)):
        freqs = 10000.0 ** (-np.arange(count) / count)
        angle = np.arange(GRID)[:, None] * freqs[None]
        table[section, :, begin : begin + count] = np.cos(angle)
        table[section, :, HALF + begin : HALF + begin + count] = np.sin(angle)
        begin += count
    rest = table.reshape(3 * GRID, HEAD_DIM)
    terms = []
    for _ in range(3):
        terms.append(rest.astype(np.float32).astype(jnp.bfloat16))
        rest = rest - terms[-1].astype(np.float64)
    return np.concatenate(terms, axis=1)


def dot(left, right, contract):
    return lax.dot_general(left, right, ((contract[0], contract[1]), ((), ())), preferred_element_type=F32)


def rotary(rows, table):
    tokens = rows[0].shape[1]
    terms = dot(picks_of(rows), table, ((0,), (0,)))
    both = terms[:, :HEAD_DIM] + terms[:, HEAD_DIM : 2 * HEAD_DIM] + terms[:, 2 * HEAD_DIM :]
    other = pltpu.roll(both, HALF, 1)
    lower = lax.broadcasted_iota(jnp.int32, (tokens, HEAD_DIM), 1) < HALF
    return jnp.where(lower, both, other), jnp.where(lower, -other, both)


def double_table():
    sixth = HEAD_DIM // 6
    first = HALF - 2 * sixth
    table = np.zeros((3, GRID, 2, 2, HALF))
    begin = 0
    for section, count in enumerate((first, sixth, sixth)):
        angle = 2 * np.arange(GRID)[:, None] * 10000.0 ** (-np.arange(count) / count)[None]
        at = slice(begin, begin + count)
        table[section, :, 0, 0, at], table[section, :, 0, 1, at] = np.cos(angle), -np.cos(angle)
        table[section, :, 1, 0, at] = table[section, :, 1, 1, at] = np.sin(angle)
        begin += count
    table = table.reshape(3 * GRID, 2 * HEAD_DIM)
    high = table.astype(np.float32).astype(jnp.bfloat16)
    return np.concatenate([high, (table - high.astype(np.float64)).astype(np.float32).astype(jnp.bfloat16)], axis=1)


def picks_of(rows):
    number = lax.broadcasted_iota(jnp.int32, (GRID, rows[0].shape[1]), 0).astype(F32)
    return jnp.concatenate([jnp.where(number == row, 1.0, 0.0) for row in rows], axis=0).astype(BF16)


def columns(block):
    return pl.ds(pl.multiple_of(block * HEAD_DIM, HEAD_DIM), HEAD_DIM)


def send_kernel(head, q_hbm, k_hbm, v_hbm, g_hbm, qg_hbm, kg_hbm, pos_hbm, table_hbm, *rest):
    if head == 0:
        out_hbm, aside_ref, raw, gains, pos_ref, table_ref, stage, in_sem, small_sem, out_sem = rest
    else:
        aside_ref, out_hbm, raw, gains, stage, in_sem, small_sem, out_sem = rest
    tokens, feature = q_hbm.shape
    members = out_hbm.shape[0]
    local = feature // members // HEAD_DIM
    sources = [(qg_hbm, gains.at[0]), (kg_hbm, gains.at[1])]
    if head == 0:
        sources += [(pos_hbm, pos_ref), (table_hbm, table_ref)]
    small = [pltpu.make_async_copy(source, target, small_sem.at[a]) for a, (source, target) in enumerate(sources)]
    reads = [pltpu.make_async_copy(ref, raw.at[a], in_sem.at[a]) for a, ref in enumerate((q_hbm, k_hbm, v_hbm, g_hbm))]
    for copy in small + reads:
        copy.start()
    for copy in small:
        copy.wait()
    if head == 0:
        rows = [pos_ref[a].astype(F32) for a in range(3)]
        aside_ref[0], aside_ref[1] = rotary(rows, table_ref[...])
        place = jnp.concatenate(rows + [jnp.zeros((13, tokens), F32)], axis=0).astype(BF16)
    for a in range(2):
        reads[a].wait()
        if head == 0:
            total = jnp.zeros((tokens, HEAD_DIM), F32)
            for h in range(feature // HEAD_DIM):
                part = raw[a, :, h * HEAD_DIM : (h + 1) * HEAD_DIM].astype(F32)
                total = total + part * part
            scale = lax.rsqrt(jnp.sum(total, axis=-1, keepdims=True) / feature + EPSILON)
            aside_ref[2 + a] = jnp.broadcast_to(scale, (tokens, HEAD_DIM))
    reads[2].wait()
    reads[3].wait()
    packets = []
    group = members // out_sem.shape[0]
    for j in range(members):
        at = slice((j * local + head) * HEAD_DIM, (j * local + head + 1) * HEAD_DIM)
        for a in range(2):
            x = raw[a, :, at].astype(F32) * aside_ref[2 + a] * gains[a, :, at]
            turned = x * aside_ref[0] + pltpu.roll(x, HALF, 1) * aside_ref[1]
            stage[j, a * tokens : (a + 1) * tokens, :] = turned.astype(BF16)
        for a in (2, 3):
            stage[j, a * tokens : (a + 1) * tokens, :] = raw[a, :, at]
        if head == 0:
            stage[j, SLAB:, :] = place
        if j % group == group - 1:
            some = slice(j + 1 - group, j + 1)
            packets.append(pltpu.make_async_copy(stage.at[some], out_hbm.at[some], out_sem.at[j // group]))
            packets[-1].start()
    for copy in packets:
        copy.wait()


def attention_kernel(head, len_ref, x_ref, *rest):
    if head == 0:
        table_ref, out_hbm, sum_ref, angles_hbm, *rest = rest
    else:
        angles_hbm, before_ref, out_hbm, sum_ref, *rest = rest
    out_ref, qt, kt, vt, gt, keymask, dk, dv, angles, out_sem, angle_sem = rest
    members = x_ref.shape[0]
    tok = HEAD_DIM
    tokens = members * tok
    local = 1
    clips = len_ref.shape[0]
    scale = HEAD_DIM ** (-0.5)
    factor = scale * math.log2(math.e)

    group = members // out_sem.shape[0]
    if head == 0:
        hand = pltpu.make_async_copy(angles, angles_hbm, angle_sem)
    else:
        hand = pltpu.make_async_copy(angles_hbm, angles, angle_sem)
        hand.start()
    ends = []
    so_far = 0
    for c in range(clips):
        so_far = so_far + len_ref[c]
        ends.append(so_far)

    def masks(i, carry):
        token = lax.broadcasted_iota(jnp.int32, (tok, HEAD_DIM), 0) + i * tok
        lane = lax.broadcasted_iota(jnp.int32, (tok, HEAD_DIM), 1)
        clip = jnp.zeros((tok, HEAD_DIM), jnp.int32)
        for c in range(clips):
            clip = clip + (token >= ends[c]).astype(jnp.int32)
        own = clip == lane
        at = pl.ds(pl.multiple_of(i * tok, tok), tok)
        keymask[at, :] = jnp.where(own, -APART, 0.0).astype(BF16)
        token = lax.broadcasted_iota(jnp.int32, (HEAD_DIM, tok), 1) + i * tok
        lane = lax.broadcasted_iota(jnp.int32, (HEAD_DIM, tok), 0)
        clip = jnp.zeros((HEAD_DIM, tok), jnp.int32)
        for c in range(clips):
            clip = clip + (token >= ends[c]).astype(jnp.int32)
        apart = jnp.where(clip == lane, 0.0, 1.0).astype(BF16)
        if head == 0:
            rows = x_ref[i, SLAB:, :].astype(F32)
            terms = dot(picks_of([rows[a : a + 1] for a in range(3)]), table_ref[...], ((0,), (0,)))
            angles[at, :] = terms[:, : 2 * HEAD_DIM] + terms[:, 2 * HEAD_DIM :]
        for h in range(local):
            qt[h, :HEAD_DIM, at] = x_ref[i, h * SLAB : h * SLAB + tok, :].T
            qt[h, HEAD_DIM:, at] = apart
            gt[h, :, at] = x_ref[i, h * SLAB + 3 * tok : h * SLAB + 4 * tok, :].T
            kt[h, :, at] = x_ref[i, h * SLAB + tok : h * SLAB + 2 * tok, :].T
            vt[h, :, at] = x_ref[i, h * SLAB + 2 * tok : h * SLAB + 3 * tok, :].T
            dk[h, at, :] = jnp.zeros((tok, HEAD_DIM), F32)
            dv[h, at, :] = jnp.zeros((tok, HEAD_DIM), F32)
        return carry

    lax.fori_loop(0, members, masks, 0)
    if head == 0:
        hand.start()

    per = QUERY_TILE // tok
    step = KEY_STEP // tok

    def window(i):
        first, last = jnp.int32(0), jnp.int32(tokens)
        for c in range(clips):
            first = jnp.where(ends[c] <= i * QUERY_TILE, ends[c], first)
        for c in reversed(range(clips)):
            last = jnp.where(ends[c] >= (i + 1) * QUERY_TILE, ends[c], last)
        low = first // tok
        return low, (last - low * tok + KEY_STEP - 1) // KEY_STEP

    def block(a, start, number):
        return x_ref[pl.ds(start, number), a * tok : (a + 1) * tok, :].reshape(number * tok, HEAD_DIM)

    def pair(i, carry):
        tiles = (2 * i, 2 * i + 1)
        windows = [window(t) for t in tiles]
        count = jnp.maximum(windows[0][1], windows[1][1])
        q_at = [pl.ds(pl.multiple_of(t * QUERY_TILE, QUERY_TILE), QUERY_TILE) for t in tiles]

        def whole(number):
            both = range(2)
            k0 = [[jnp.minimum(windows[t][0], members - number * step) + j * step for j in range(number)] for t in both]
            k_at = [[pl.ds(pl.multiple_of(k * tok, tok), KEY_STEP) for k in k0[t]] for t in both]
            s, highest = {}, {}
            for j in range(number):
                for t in both:
                    keys = jnp.concatenate([block(1, k0[t][j], step), keymask[k_at[t][j], :]], axis=1)
                    s[t, j] = dot(keys, qt[0, :, q_at[t]], ((1,), (0,)))
                    m = jnp.max(s[t, j].reshape(KEY_STEP // 8, 8, QUERY_TILE), axis=0)
                    highest[t] = m if j == 0 else jnp.maximum(highest[t], m)
            e, total, out = {}, {}, {}
            for t in both:
                top = jnp.max(highest[t], axis=0, keepdims=True)
                for j in range(number):
                    e[t, j] = jnp.exp2((s[t, j] - top) * factor)
                    n = jnp.sum(e[t, j].reshape(KEY_STEP // 8, 8, QUERY_TILE), axis=0)
                    o = dot(vt[0, :, k_at[t][j]], e[t, j].astype(BF16), ((1,), (0,)))
                    total[t] = n if j == 0 else total[t] + n
                    out[t] = o if j == 0 else out[t] + o
            for t in both:
                rows = pl.ds(tiles[t] * per, per)
                inv = 1.0 / jnp.sum(total[t], axis=0, keepdims=True)
                attended = (out[t] * inv).astype(BF16)
                delta = jnp.sum(attended.astype(F32) * gt[0, :, q_at[t]].astype(F32), axis=0, keepdims=True)
                out_ref[rows, :tok, :] = attended.T.reshape(per, tok, HEAD_DIM)
                query, cot = block(0, tiles[t] * per, per), block(3, tiles[t] * per, per)
                for j in range(number):
                    prob = e[t, j] * inv
                    dprob = dot(block(2, k0[t][j], step), gt[0, :, q_at[t]], ((1,), (0,)))
                    dscore = (prob * (dprob - delta)).astype(BF16)
                    dv[0, k_at[t][j], :] += dot(prob.astype(BF16), cot, ((1,), (0,)))
                    dk[0, k_at[t][j], :] += dot(dscore, query, ((1,), (0,)))
                    d = dot(kt[0, :, k_at[t][j]], dscore, ((1,), (0,)))
                    dq = d if j == 0 else dq + d
                out_ref[rows, tok : 2 * tok, :] = (dq * scale).astype(BF16).T.reshape(per, tok, HEAD_DIM)

        for number in range(1, tokens // KEY_STEP + 1):

            @pl.when(count == number)
            def _():
                whole(number)

        return carry

    lax.fori_loop(0, tokens // QUERY_TILE // 2, pair, 0)

    hand.wait()

    def write(n):
        some = pl.ds(n * group, group)
        return pltpu.make_async_copy(out_ref.at[some], out_hbm.at[some, :SLAB, :], out_sem.at[n])

    def finish(i, sums):
        at = pl.ds(pl.multiple_of(i * tok, tok), tok)
        cosine, sine = angles[at, :HEAD_DIM], angles[at, HEAD_DIM:]
        new = []
        for h in range(local):
            dk_tile = (dk[h, at, :] * scale).astype(BF16)
            out_ref[i, h * SLAB + 2 * tok : h * SLAB + 3 * tok, :] = dk_tile
            out_ref[i, h * SLAB + 3 * tok : h * SLAB + 4 * tok, :] = dv[h, at, :].astype(BF16)

        @pl.when(lax.rem(i, group) == group - 1)
        def _():
            write(i // group).start()

        for h in range(local):
            for a, row in ((0, 1), (1, 2)):
                g = out_ref[i, h * SLAB + row * tok : h * SLAB + (row + 1) * tok, :].astype(F32)
                p = x_ref[i, h * SLAB + a * tok : h * SLAB + (a + 1) * tok, :].astype(F32)
                straight = g * p
                across = straight * cosine + g * pltpu.roll(p, HALF, 1) * sine
                plain, turned = sums[2 * h + a]
                new.append(
                    (
                        plain + jnp.sum(straight.reshape(tok // 8, 8, HEAD_DIM), axis=0),
                        turned + jnp.sum(across.reshape(tok // 8, 8, HEAD_DIM), axis=0),
                    )
                )
        return tuple(new)

    zero = jnp.zeros((8, HEAD_DIM), F32)
    sums = lax.fori_loop(0, members, finish, ((zero, zero),) * (2 * local))
    fill = [jnp.zeros((8 - 2, HEAD_DIM), F32)]
    plain, turned = (
        jnp.concatenate([jnp.sum(s[n], axis=0, keepdims=True) for s in sums] + fill, axis=0) for n in range(2)
    )
    plain = plain + pltpu.roll(plain, HALF, 1)
    turned = turned + pltpu.roll(turned, HALF, 1)
    lower = lax.broadcasted_iota(jnp.int32, plain.shape, 1) < HALF
    sums = 0.5 * (plain + jnp.where(lower, turned, -turned))
    if head > 0:
        sums = jnp.concatenate([before_ref[: 2 * head], sums[: 8 - 2 * head]], axis=0)
    sum_ref[...] = sums
    for n in range(members // group):
        write(n).wait()


def insert_kernel(sum_ref, y_hbm, out_hbm, rows_ref, sem):
    del y_hbm
    rest = sum_ref[:4]
    terms = []
    for _ in range(3):
        terms.append(rest.astype(BF16).astype(F32))
        rest = rest - terms[-1]
    rows_ref[...] = jnp.concatenate(terms + [jnp.zeros_like(rest)], axis=0).astype(BF16)
    number = rows_ref.shape[0]
    copies = [
        pltpu.make_async_copy(rows_ref, out_hbm.at[i, SLAB : SLAB + number, :], sem.at[i])
        for i in range(out_hbm.shape[0])
    ]
    for copy in copies:
        copy.start()
    for copy in copies:
        copy.wait()


def spread_copies(j, head, local, y_ref, att_hbm, gv_hbm, sem):
    tokens = att_hbm.shape[0]
    at = slice((j * local + head) * HEAD_DIM, (j * local + head + 1) * HEAD_DIM)
    return [
        pltpu.make_async_copy(y_ref.at[j, row * tokens : (row + 1) * tokens, :], ref.at[:, at], sem.at[j, a])
        for a, (ref, row) in enumerate(((att_hbm, 0), (gv_hbm, 3)))
    ]


def early_kernel(local, y_ref, q_ref, k_ref, qg_ref, kg_ref, aside_ref, att_hbm, gv_hbm, lift_hbm, total_ref, lift_ref, spread_sem, lift_sem):
    tokens = q_ref.shape[0]
    members = y_ref.shape[0]
    copies = []
    for j in range(members):
        copies += spread_copies(j, 0, local, y_ref, att_hbm, gv_hbm, spread_sem)
    for copy in copies:
        copy.start()
    for a, (raw_ref, gain_ref) in enumerate(((q_ref, qg_ref), (k_ref, kg_ref))):
        total = jnp.zeros((tokens, HEAD_DIM), F32)
        for j in range(members):
            at = slice(j * local * HEAD_DIM, (j * local + 1) * HEAD_DIM)
            g = y_ref[j, (a + 1) * tokens : (a + 2) * tokens, :].astype(F32)
            g = g * aside_ref[0] - pltpu.roll(g, HALF, 1) * aside_ref[1]
            lift = g * gain_ref[:, at]
            lift_ref[a, :, j * HEAD_DIM : (j + 1) * HEAD_DIM] = lift
            total = total + lift * (raw_ref[:, at].astype(F32) * aside_ref[2 + a])
        total_ref[a] = total
        copies.append(pltpu.make_async_copy(lift_ref.at[a], lift_hbm.at[a], lift_sem.at[a]))
        copies[-1].start()
    for copy in copies:
        copy.wait()


def receive_kernel(buckets, yb_hbm, q_ref, k_ref, qg_ref, kg_ref, aside, lift_hbm, totals, att_in, gv_in, gq_hbm, gk_hbm, gqg_ref, gkg_ref, att_hbm, gv_hbm, yb, before, lift_ref, stage, lift_sem, y_sem, spread_sem, sem):
    del att_in, gv_in
    raw, gains = (q_ref, k_ref), (qg_ref, kg_ref)
    tokens, feature = q_ref.shape
    members = yb_hbm.shape[0]
    local = feature // members // HEAD_DIM
    groups = y_sem.shape[0]
    group = members // groups
    def arrive(n):
        some = slice(n * group, (n + 1) * group)
        return pltpu.make_async_copy(yb_hbm.at[some], yb.at[some], y_sem.at[n])

    for n in range(groups):
        arrive(n).start()
    lifts = [pltpu.make_async_copy(lift_hbm.at[a], before.at[a], lift_sem.at[a]) for a in range(2)]
    for copy in lifts:
        copy.start()
    copies = []
    parts = sem.shape[1]
    width = feature // parts
    number = 2 * local
    for a, grad_hbm in enumerate((gq_hbm, gk_hbm)):
        total = totals[a]
        for j in range(members):
            if a == 0 and j % group == 0:
                arrive(j // group).wait()
                for n in range(j, j + group):
                    spread = spread_copies(n, 1, local, yb, att_hbm, gv_hbm, spread_sem)
                    for copy in spread:
                        copy.start()
                    copies += spread
            at = slice((j * local + 1) * HEAD_DIM, (j * local + 2) * HEAD_DIM)
            g = yb[j, (a + 1) * tokens : (a + 2) * tokens, :].astype(F32)
            g = g * aside[0] - pltpu.roll(g, HALF, 1) * aside[1]
            lift = g * gains[a][:, at]
            lift_ref[a, :, j * HEAD_DIM : (j + 1) * HEAD_DIM] = lift
            total = total + lift * (raw[a][:, at].astype(F32) * aside[2 + a])
        inner = jnp.sum(total, axis=-1, keepdims=True) / feature
        lifts[a].wait()
        lean = jnp.broadcast_to(inner, (tokens, HEAD_DIM)) * aside[2 + a]
        for part in range(parts):
            for block in range(part * width // HEAD_DIM, (part + 1) * width // HEAD_DIM):
                at = slice(block * HEAD_DIM, (block + 1) * HEAD_DIM)
                j, h = divmod(block, local)
                lift = (before, lift_ref)[h][a, :, j * HEAD_DIM : (j + 1) * HEAD_DIM]
                stage[a, :, at] = (aside[2 + a] * (lift - raw[a][:, at].astype(F32) * lean)).astype(BF16)
            at = slice(part * width, (part + 1) * width)
            copies.append(pltpu.make_async_copy(stage.at[a, :, at], grad_hbm.at[:, at], sem.at[a, part]))
            copies[-1].start()
    for j in range(members):
        rows = yb[j, SLAB:, :].astype(F32)
        total = rows[:number] + rows[number : 2 * number] + rows[2 * number : 3 * number]
        for h in range(local):
            at = slice((j * local + h) * HEAD_DIM, (j * local + h + 1) * HEAD_DIM)
            gqg_ref[:, at] = total[2 * h : 2 * h + 1] / (gains[0][:, at] * buckets)
            gkg_ref[:, at] = total[2 * h + 1 : 2 * h + 2] / (gains[1][:, at] * buckets)
    for copy in copies:
        copy.wait()


def on_device(q_raw, k_raw, values, grad_out, q_gain, k_gain, lengths, positions):
    members = lax.axis_size("seq")
    replicas = lax.axis_size("dp")
    _, tok, feature = q_raw.shape
    local = feature // members // HEAD_DIM
    tokens = tok * members
    vmem = pl.BlockSpec(memory_space=pltpu.VMEM)
    smem = pl.BlockSpec(memory_space=pltpu.SMEM)
    hbm = pl.BlockSpec(memory_space=pltpu.HBM)
    sems = pltpu.SemaphoreType.DMA
    table = jnp.asarray(rotary_table())
    doubled = jnp.asarray(double_table())
    shape = jax.ShapeDtypeStruct
    slabs = shape((members, SLAB, HEAD_DIM), BF16)
    longer = shape((members, SLAB + 16, HEAD_DIM), BF16)
    row_shape = shape((tok, feature), BF16)

    def send(head, aside):
        first = head == 0
        packet = longer if first else slabs
        scratch = [pltpu.VMEM((4, tok, feature), BF16), pltpu.VMEM((2, 1, feature), F32)]
        if first:
            scratch += [pltpu.VMEM((3, 1, tok), jnp.int32), pltpu.VMEM(table.shape, BF16)]
        return pl.pallas_call(
            functools.partial(send_kernel, head),
            out_shape=(packet, shape((4, tok, HEAD_DIM), F32)) if first else packet,
            in_specs=[hbm] * 8 + ([] if first else [vmem]),
            out_specs=(hbm, vmem) if first else hbm,
            scratch_shapes=scratch + [pltpu.VMEM(packet.shape, BF16), sems((4,)), sems((4,)), sems((4,))],
            compiler_params=pltpu.CompilerParams(vmem_limit_bytes=60 << 20),
            cost_estimate=pl.CostEstimate(flops=20 << 20, bytes_accessed=6 << 20, transcendentals=0),
            name="send",
        )(
            *(a[0] for a in (q_raw, k_raw, values, grad_out)),
            q_gain[None],
            k_gain[None],
            jnp.transpose(positions, (1, 0, 2)),
            table,
            *([] if first else [aside]),
        )

    def exchange(packet):
        return lax.all_to_all(packet, "seq", 0, 0, tiled=True)

    angle_shape = shape((tokens, 2 * HEAD_DIM), F32)

    def attend(head, got, *others):
        first = head == 0
        outs = (longer if head == local - 1 else slabs, shape((8, HEAD_DIM), F32))
        return pl.pallas_call(
            functools.partial(attention_kernel, head),
            out_shape=outs + ((angle_shape,) if first else ()),
            in_specs=[smem, vmem] + ([vmem] if first else [hbm, vmem]),
            out_specs=(hbm, vmem) + ((hbm,) if first else ()),
            scratch_shapes=[
                pltpu.VMEM((members, SLAB, HEAD_DIM), BF16),
                pltpu.VMEM((1, 2 * HEAD_DIM, tokens), BF16),
                pltpu.VMEM((1, HEAD_DIM, tokens), BF16),
                pltpu.VMEM((1, HEAD_DIM, tokens), BF16),
                pltpu.VMEM((1, HEAD_DIM, tokens), BF16),
                pltpu.VMEM((tokens, HEAD_DIM), BF16),
                pltpu.VMEM((1, tokens, HEAD_DIM), F32),
                pltpu.VMEM((1, tokens, HEAD_DIM), F32),
                pltpu.VMEM(angle_shape.shape, F32),
                sems((4,)),
                sems(()),
            ],
            compiler_params=pltpu.CompilerParams(vmem_limit_bytes=50 << 20),
            cost_estimate=pl.CostEstimate(flops=10 << 30, bytes_accessed=5 << 20, transcendentals=1 << 22),
            name="attention",
        )(lengths[0], got, *others)

    packet_a, aside = send(0, None)
    got_a = exchange(packet_a)
    packet_b = send(1, aside)
    got_b = exchange(packet_b)
    back_a, sum_a, angles = attend(0, got_a, doubled)
    y_a = exchange(back_a)
    back_b, sums = attend(1, got_b, angles, sum_a)
    for distance in (1, 2, 4):
        sums = sums + lax.ppermute(sums, "dp", [(i, i ^ distance) for i in range(replicas)])
    back_b = pl.pallas_call(
        insert_kernel,
        out_shape=longer,
        in_specs=[vmem, hbm],
        out_specs=hbm,
        scratch_shapes=[pltpu.VMEM((16, HEAD_DIM), BF16), sems((members,))],
        input_output_aliases={1: 0},
        name="insert",
    )(sums, back_b)
    y_b = exchange(back_b)
    half_shape = shape((2, tok, feature // local), F32)
    total_shape = shape((2, tok, HEAD_DIM), F32)
    attended, grad_v, lift, totals = pl.pallas_call(
        functools.partial(early_kernel, local),
        out_shape=(row_shape, row_shape, half_shape, total_shape),
        in_specs=[vmem] * 6,
        out_specs=(hbm, hbm, hbm, vmem),
        scratch_shapes=[pltpu.VMEM(half_shape.shape, F32), sems((members, 2)), sems((2,))],
        compiler_params=pltpu.CompilerParams(vmem_limit_bytes=60 << 20),
        cost_estimate=pl.CostEstimate(flops=20 << 20, bytes_accessed=6 << 20, transcendentals=0),
        name="early",
    )(y_a, q_raw[0], k_raw[0], q_gain[None], k_gain[None], aside)
    grad_q, grad_k, q_sum, k_sum, attended, grad_v = pl.pallas_call(
        functools.partial(receive_kernel, replicas),
        out_shape=(row_shape, row_shape, shape((1, feature), F32), shape((1, feature), F32), row_shape, row_shape),
        in_specs=[hbm] + [vmem] * 5 + [hbm, vmem] + [hbm] * 2,
        out_specs=(hbm, hbm, vmem, vmem, hbm, hbm),
        scratch_shapes=[
            pltpu.VMEM(longer.shape, BF16),
            pltpu.VMEM(half_shape.shape, F32),
            pltpu.VMEM(half_shape.shape, F32),
            pltpu.VMEM((2, tok, feature), BF16),
            sems((2,)),
            sems((4,)),
            sems((members, 2)),
            sems((2, 4)),
        ],
        input_output_aliases={8: 4, 9: 5},
        compiler_params=pltpu.CompilerParams(vmem_limit_bytes=24 << 20),
        cost_estimate=pl.CostEstimate(flops=40 << 20, bytes_accessed=8 << 20, transcendentals=0),
        name="receive",
    )(y_b, q_raw[0], k_raw[0], q_gain[None], k_gain[None], aside, lift, totals, attended, grad_v)
    return tuple(o[None] for o in (attended, grad_q, grad_k, grad_v)) + (q_sum[0], k_sum[0])


def solution(mesh):
    tokens_split = P("dp", "seq", None)
    return jax.shard_map(
        on_device,
        mesh=mesh,
        in_specs=(tokens_split,) * 4 + (P(), P(), P("dp", None), P("dp", None, "seq")),
        out_specs=(tokens_split,) * 4 + (P(), P()),
        check_vma=False,
    )
```
